512 devices in a mesh: sens: 32 (over y, x), tm: 16 (over z, core).
Axes of the slice: x: 4, y: 8, z: 8, core: 2. Of those that a mesh axis runs over, the one named last changes fastest.
Arguments:
- observed: float32 [64, 16384], P('tm', 'sens'), may hold values from -16 to 16
- loadings: bfloat16 [16384, 512], P('sens'), may hold values from -0.046875 to 0.046875
- noise_prec: float32 [16384], P('sens'), may hold values from 0.02 to 0.2
- dynamics: float32 [512, 512], replicated, as said below
- prior_prec: float32 [512, 512], replicated, as said below
Outputs:
- filtered: float32 [64, 512], P('tm')
- smoothed: float32 [64, 512], P('tm')
The draws below stay inside these ranges and needn't reach their ends.
Inputs may be any that keep to these rules, and one draw needn't show every extreme that they name: `dynamics`: a real square transition matrix. `prior_prec`: symmetric positive definite; commutes with dynamics.
All inputs are finite; a program needn't handle non-finite values.
Results may differ from the reference program's by a relative error of at most 0.0003.
Values sent between devices are 32-bit elements; how exact they have to be, the bound alone decides.
No kernel may reach another device: no remote copies, remote signals or barrier semaphores. Data moves between devices by JAX's collectives and lax.ppermute only.
A program may use at most 64 MiB of HBM per device.

```python
import math
import jax
import jax.numpy as jnp
from jax import lax

R = 512
M = 16384
TSTEPS = 64


def dynamics_pair(key):
    noise_mat = jax.random.normal(jax.random.fold_in(key, 31), (R, R), jnp.float32)
    skew_part = (noise_mat - noise_mat.T) / jnp.sqrt(jnp.float32(2 * R))
    rotate_rate, radius, slope_prec = (0.12, 0.995, 4.0)
    identity = jnp.eye(R, dtype=jnp.float32)
    rotation = jnp.linalg.solve(identity - rotate_rate * skew_part, identity + rotate_rate * skew_part)
    square_part = jnp.dot(skew_part.T, skew_part, precision=lax.Precision.HIGHEST)
    return (radius * rotation, identity + slope_prec * square_part)


def draw_dynamics(key, part):
    return dynamics_pair(key)[0]


def draw_prior_prec(key, part):
    return dynamics_pair(key)[1]


def level_of(stream_key, dims, split, smallest, high):
    level, own = 1.0, jax.random.fold_in(stream_key, 6)
    for axis_at, blocks in split:
        steps = jnp.exp(jax.random.uniform(jax.random.fold_in(own, axis_at), (blocks,), jnp.float32, smallest / len(split), high / len(split)))
        level = level * jnp.repeat(steps, dims[axis_at] // blocks).reshape([-1 if axis == axis_at else 1 for axis in range(len(dims))])
    return level


def noise(rng, shape, width, reach, pieces=(), held_as=jnp.bfloat16):
    entries = jax.random.normal(rng, shape, jnp.float32) * width
    if len(pieces) > 0:
        entries = level_of(rng, shape, pieces, -0.22, 0.18) * entries
    return jnp.clip(entries, min=-reach, max=reach).astype(held_as)


def setup_inputs(seed: int = 0) -> dict:
    key_of = jax.random.split(jax.random.key(seed), 6)
    observed = noise(key_of[0], (TSTEPS, M), 4.0, 16.0, ((0, 16), (1, 32)), jnp.float32)
    loadings = noise(key_of[1], (M, R), M ** -0.5, 0.046875, ((0, 32),))
    noise_prec = jnp.clip(jnp.exp(math.log(0.2) - 2.3025851 * jax.random.uniform(key_of[2], (M,), jnp.float32) ** level_of(key_of[2], (M,), ((0, 32),), -0.2, 0.2)), 0.02, 0.2)
    dynamics = draw_dynamics(jax.random.fold_in(key_of[5], 71), 0)
    prior_prec = draw_prior_prec(jax.random.fold_in(key_of[5], 71), 0)
    return {"observed": observed, "loadings": loadings, "noise_prec": noise_prec, "dynamics": dynamics, "prior_prec": prior_prec}


precise = lax.Precision.HIGHEST

def inverse_spd(matrix):
    lower_factor = jnp.linalg.cholesky(matrix)
    identity = jnp.eye(matrix.shape[0], dtype=matrix.dtype)
    lower_inv = lax.linalg.triangular_solve(lower_factor, identity, left_side=True, lower=True)
    return jnp.dot(lower_inv.T, lower_inv, precision=precise)

def model_mats(gram_mat, prior_prec, dynamics):
    post_cov = inverse_spd(gram_mat + prior_prec)
    forward = jnp.dot(post_cov, jnp.dot(prior_prec, dynamics, precision=precise), precision=precise)
    gain_mat = jnp.dot(post_cov, jnp.dot(dynamics.T, prior_prec, precision=precise), precision=precise)
    identity = jnp.eye(gram_mat.shape[0], dtype=gram_mat.dtype)
    keep_mat = identity - jnp.dot(gain_mat, dynamics, precision=precise)
    return (post_cov, forward, gain_mat, keep_mat)

def reference(observed, loadings, noise_prec, dynamics, prior_prec):
    load_rows = loadings.astype(jnp.float32)
    gram_mat = jnp.dot((load_rows * noise_prec[:, None]).T, load_rows, precision=precise)
    info_rows = jnp.dot(observed * noise_prec[None, :], load_rows, precision=precise)
    post_cov, forward, gain_mat, keep_mat = model_mats(gram_mat, prior_prec, dynamics)
    drive_rows = jnp.dot(info_rows, post_cov.T, precision=precise)
    run_state = jnp.zeros((gram_mat.shape[0],), jnp.float32)
    filt_rows = []
    for time_step in range(TSTEPS):
        run_state = jnp.dot(forward, run_state, precision=precise) + drive_rows[time_step]
        filt_rows.append(run_state)
    smooth = jnp.dot(dynamics, filt_rows[-1], precision=precise)
    smooth_rows = [None] * TSTEPS
    for time_step in range(TSTEPS - 1, -1, -1):
        smooth = jnp.dot(keep_mat, filt_rows[time_step], precision=precise) + jnp.dot(gain_mat, smooth, precision=precise)
        smooth_rows[time_step] = smooth
    return (jnp.stack(filt_rows), jnp.stack(smooth_rows))
```

```python
from functools import partial

import jax
import jax.numpy as jnp
from jax import lax
from jax.experimental import pallas as pl
from jax.experimental.pallas import tpu as pltpu
from jax.sharding import PartitionSpec as P

f32 = jnp.float32
bf16 = jnp.bfloat16
R = 512


def dot1(a, b, ca=1, cb=0):
    return lax.dot_general(a, b, (((ca,), (cb,)), ((), ())), preferred_element_type=f32)


def split(a):
    hi = a.astype(bf16)
    return hi, (a - hi.astype(f32)).astype(bf16)


def dot3(a, b, ca=1, cb=0):
    return dot1(a[0], b[0], ca, cb) + (dot1(a[0], b[1], ca, cb) + dot1(a[1], b[0], ca, cb))


def dot6(a, b, ca=1, cb=0):
    return lax.dot_general(
        a, b, (((ca,), (cb,)), ((), ())), precision=lax.Precision.HIGHEST, preferred_element_type=f32
    )


def eye():
    return (lax.broadcasted_iota(jnp.int32, (R, R), 0) == lax.broadcasted_iota(jnp.int32, (R, R), 1)).astype(f32)


def sum_sq(x):
    return jnp.sum(x * x)


def sweep_inverse(ref):
    lane = lax.broadcasted_iota(jnp.int32, (1, R), 1)
    row_at = lax.broadcasted_iota(jnp.int32, (R, 1), 0)

    def body(k, _):
        a = ref[...]
        row = ref[pl.ds(k, 1), :]
        here = lane == k
        pivot = jnp.sum(jnp.where(here, row, 0.0), axis=1, keepdims=True)
        col = jnp.sum(jnp.where(here, a, 0.0), axis=1, keepdims=True)
        col = jnp.where(row_at == k, 0.0, col)
        row = jnp.where(here, 1.0, row) / pivot
        ref[...] = jnp.where(here, 0.0, a) - col * row
        ref[pl.ds(k, 1), :] = row
        return 0

    lax.fori_loop(0, R, body, 0)


ROWS = 24
INFO = 640


def partials(tm_ref, obs_ref, load_ref, noise_ref, out_ref):
    noise = noise_ref[...]
    column = jnp.broadcast_to(noise, (128, R)).T

    def weighted(i):
        return split(load_ref[:, 128 * i : 128 * i + 128].astype(f32) * column)

    def pairs(i, lo, at):
        rows = load_ref[:, lo:]
        hi, rest = weighted(i)
        blocks = dot1(hi, rows, 0, 0) + dot1(rest, rows, 0, 0)
        for n in range((R - lo) // 128):
            out_ref[at + 128 * n : at + 128 * n + 128, :] = blocks[:, 128 * n : 128 * n + 128]

    def one(i, at):
        rows = load_ref[:, 128 * i : 128 * i + 128]
        hi, rest = weighted(i)
        out_ref[at : at + 128, :] = dot1(hi, rows, 0, 0) + dot1(rest, rows, 0, 0)

    first = lax.rem(tm_ref[0], 2) == 0

    @pl.when(first)
    def _():
        pairs(0, 0, 0)
        one(1, 512)

    @pl.when(jnp.logical_not(first))
    def _():
        pairs(1, 256, 0)
        pairs(2, 256, 256)
        one(3, 512)

    hi, rest = split(obs_ref[...] * noise)
    rows = load_ref[...]
    info = dot1(hi, rows) + dot1(rest, rows)
    for t in range(4):
        for c in range(4):
            out_ref[INFO + 4 * t + c : INFO + 4 * t + c + 1, :] = info[t : t + 1, 128 * c : 128 * c + 128]
    out_ref[INFO + 16 :, :] = jnp.zeros((32 * ROWS - INFO - 16, 128), f32)


def sum_and_spread(in_ref, out_ref):
    total = in_ref[0]
    for n in range(1, 32):
        total = total + in_ref[n]
    for n in range(32):
        out_ref[n] = total


def prep_a(dyn_ref, prior_ref, wt_ref, nn_ref, x_ref):
    prior = prior_ref[...]
    psplit = split(prior)
    wt = dot6(dyn_ref[...], prior, 0, 0)
    wt_ref[...] = wt
    nn_ref[...] = dot6(wt, dyn_ref[...])
    col = jnp.sum(jnp.abs(prior), axis=0, keepdims=True)
    start = 1.0 / jnp.max(col, axis=1, keepdims=True)
    ident = eye()
    x = ident * start
    ph = psplit[0]
    x = start * (2.0 * ident - start * prior)
    x_ref[...] = x

    def body(k, _):
        x = x_ref[...]
        xh = x.astype(bf16)
        t = dot1(ph, xh)
        x_ref[...] = 2.0 * x - dot1(xh, t.astype(bf16))
        return 0

    lax.fori_loop(0, 6, body, 0)


def refine(times_mat, x_ref, r_ref, done2, cap):
    ident = eye()

    def residual():
        r = ident - times_mat(x_ref[...])
        r_ref[...] = r
        return sum_sq(r)

    def cond(c):
        k, n2, old = c
        return (n2 > done2) & (k < cap) & (n2 < 0.98 * old)

    def body(c):
        k, n2, _ = c
        x = x_ref[...]
        x_ref[...] = x + dot3(split(x), split(r_ref[...]))
        return k + 1, residual(), n2

    n0 = residual()
    return lax.while_loop(cond, body, (jnp.int32(0), n0, jnp.float32(jnp.inf)))


def prep_b(prior_ref, x_in, x_ref, r_ref):
    x_ref[...] = x_in[...]
    _, n2, _ = refine(lambda v: dot3(split(prior_ref[...]), split(v)), x_ref, r_ref, 1e-5, 40)

    @pl.when(jnp.logical_not(n2 < 0.05))
    def _():
        x_ref[...] = prior_ref[...]
        sweep_inverse(x_ref)


PAIRS = ((0, 0), (0, 1), (0, 2), (0, 3), (1, 1), (1, 2), (1, 3), (2, 2), (2, 3), (3, 3))


def invert(tm_ref, own_ref, other_ref, prior_ref, pinv_ref, wt_ref, a_ref, x_ref, ft_ref, g_ref, r_ref):
    first = lax.rem(tm_ref[0], 2) == 0
    for n, (i, j) in enumerate(PAIRS):
        at = (n % 5) * 128
        mine, theirs = own_ref[at : at + 128, :], other_ref[at : at + 128, :]
        blk = jnp.where(first, mine, theirs) if n < 5 else jnp.where(first, theirs, mine)
        g_ref[128 * i : 128 * i + 128, 128 * j : 128 * j + 128] = blk
        if i != j:
            g_ref[128 * j : 128 * j + 128, 128 * i : 128 * i + 128] = blk.T
    gram = g_ref[...]
    a = prior_ref[...] + gram
    a_ref[...] = a
    pinv = pinv_ref[...]
    ph = pinv.astype(bf16)
    e = dot1(gram.astype(bf16), ph)
    size = jnp.sqrt(sum_sq(e))
    theta = jnp.where(size < 0.9, 1.0, 2.0 / (2.0 + size))
    r0 = (1.0 - theta) * eye() - theta * e
    rh = r0.astype(bf16)
    t = dot1(rh, rh)
    s = r0 + t + dot1(rh, t.astype(bf16))
    x_ref[...] = theta * (pinv + dot1(ph, s.astype(bf16)))
    _, n2, _ = refine(lambda v: dot6(a_ref[...], v), x_ref, r_ref, 1e-4, 60)

    good = n2 < 1e-4

    @pl.when(good)
    def _():
        x = x_ref[...]
        r = r_ref[...]
        rh = r.astype(bf16)
        x_ref[...] = x + dot1(x.astype(bf16), (r + dot1(rh, rh)).astype(bf16))

    @pl.when(jnp.logical_not(good))
    def _():
        x_ref[...] = a_ref[...]
        sweep_inverse(x_ref)

    ft_ref[...] = dot6(wt_ref[...], x_ref[...])


def scans(tm_ref, info_ref, x_ref, ft_ref, a_ref, nn_ref, filt_ref, smooth_ref, f_ref, s_ref):
    T = 64
    x = split(x_ref[...])
    parts = [info_ref[pl.ds(c, T, stride=4), :] for c in range(4)]
    info = jnp.concatenate(parts, axis=1)
    y = dot3(split(info), x)
    f = ft_ref[...]
    powers = [split(f)]
    ident = eye()
    c = jnp.sum(jnp.sum(f * ident, axis=0, keepdims=True), axis=1, keepdims=True) * (1.0 / R)
    e = f - c * ident
    es = split(e)
    f = c * (f + e) + dot3(es, es)
    powers.append(split(f))
    for _ in range(4):
        f = dot3(powers[-1], powers[-1])
        powers.append(split(f))
    step = lax.broadcasted_iota(jnp.int32, (T, 1), 0)

    def later(v, k):
        return jnp.where(step >= k, pltpu.roll(v, k, 0), 0.0)

    def sooner(v, k):
        return jnp.where(step < T - k, pltpu.roll(v, T - k, 0), 0.0)

    for n, p in enumerate(powers):
        y = y + later(dot3(split(y), p), 1 << n)
    f_ref[...] = y
    nn = nn_ref[...]
    ys = split(y)
    u = dot3(ys, split(a_ref[...] - nn))
    tail = dot3(split(y[T - 8 :, :]), split(nn))
    u = u + jnp.where(step == T - 1, jnp.concatenate([jnp.zeros((T - 8, R), f32), tail], axis=0), 0.0)
    for n, p in enumerate(powers):
        u = u + sooner(dot3(split(u), p, 1, 1), 1 << n)
    s_ref[...] = dot3(split(u), x)
    at = pl.multiple_of(8 * lax.div(tm_ref[0], 2), 8)
    half = lax.rem(tm_ref[0], 2) == 0
    fb = f_ref[pl.ds(at, 8), :]
    sb = s_ref[pl.ds(at, 8), :]
    filt_ref[...] = jnp.where(half, fb[0:4], fb[4:8])
    smooth_ref[...] = jnp.where(half, sb[0:4], sb[4:8])


vm = partial(pltpu.VMEM, (R, R))
mat = jax.ShapeDtypeStruct((R, R), f32)
smem = pl.BlockSpec(memory_space=pltpu.SMEM)
vmem = pl.BlockSpec(memory_space=pltpu.VMEM)


def prep_first(dyn, prior):
    return pl.pallas_call(prep_a, out_shape=(mat, mat, mat), name="prep_a")(dyn, prior)


def prep_second(prior, x):
    return pl.pallas_call(prep_b, out_shape=mat, scratch_shapes=[vm(f32)], name="prep_b")(prior, x)


def inverse(tm, own, other, prior, pinv, wt):
    return pl.pallas_call(
        invert,
        out_shape=(mat, mat, mat),
        in_specs=[smem] + [vmem] * 5,
        scratch_shapes=[vm(f32), vm(f32)],
        name="invert",
    )(tm, own, other, prior, pinv, wt)


def time_scans(tm, info, x, ft, a, nn):
    out = jax.ShapeDtypeStruct((4, R), f32)
    return pl.pallas_call(
        scans,
        out_shape=(out, out),
        in_specs=[smem] + [vmem] * 5,
        scratch_shapes=[pltpu.VMEM((64, R), f32)] * 2,
        name="scans",
    )(tm, info, x, ft, a, nn)


def local_partials(tm, observed, loadings, noise):
    return pl.pallas_call(
        partials,
        out_shape=jax.ShapeDtypeStruct((32 * ROWS, 128), f32),
        in_specs=[smem] + [vmem] * 3,
        name="partials",
    )(tm, observed, loadings, noise)


def summed(pieces):
    return pl.pallas_call(
        sum_and_spread, out_shape=jax.ShapeDtypeStruct(pieces.shape, f32), name="sum_and_spread"
    )(pieces)


def exchange(pieces, axis):
    return lax.all_to_all(pieces, axis, split_axis=0, concat_axis=0, tiled=True)


def shards(observed, loadings, noise_prec, dynamics, prior_prec):
    tm = lax.axis_index("tm").astype(jnp.int32).reshape(1)
    send = local_partials(tm, observed, loadings, noise_prec.reshape(1, R))
    send, dynamics, prior_prec = lax.optimization_barrier((send, dynamics, prior_prec))
    pieces = exchange(send.reshape(32, ROWS, 128), "sens")
    wt, nn, x0 = prep_first(dynamics, prior_prec)
    total = summed(pieces)
    total, x0 = lax.optimization_barrier((total, x0))
    own = exchange(total, "sens").reshape(32 * ROWS, 128)
    pinv = prep_second(prior_prec, x0)
    own, pinv = lax.optimization_barrier((own, pinv))
    other = lax.ppermute(own, "tm", [(i, i ^ 1) for i in range(16)])
    info = jnp.broadcast_to(own[INFO : INFO + 16], (16, 16, 128))
    info = exchange(info, "tm").reshape(256, 128)
    a, x, ft = inverse(tm, own, other, prior_prec, pinv, wt)
    return time_scans(tm, info, x, ft, a, nn)


def solution(mesh):
    return jax.shard_map(
        shards,
        mesh=mesh,
        in_specs=(P("tm", "sens"), P("sens", None), P("sens"), P(), P()),
        out_specs=(P("tm", None), P("tm", None)),
        check_vma=False,
    )
```

```python
from functools import partial

import jax
import jax.numpy as jnp
from jax import lax
from jax.experimental import pallas as pl
from jax.experimental.pallas import tpu as pltpu
from jax.sharding import PartitionSpec as P

f32 = jnp.float32
bf16 = jnp.bfloat16
R = 512


def dot1(a, b, ca=1, cb=0):
    return lax.dot_general(a, b, (((ca,), (cb,)), ((), ())), preferred_element_type=f32)


def split(a):
    hi = a.astype(bf16)
    return hi, (a - hi.astype(f32)).astype(bf16)


def dot3(a, b, ca=1, cb=0):
    return dot1(a[0], b[0], ca, cb) + (dot1(a[0], b[1], ca, cb) + dot1(a[1], b[0], ca, cb))


def dot6(a, b, ca=1, cb=0):
    return lax.dot_general(
        a, b, (((ca,), (cb,)), ((), ())), precision=lax.Precision.HIGHEST, preferred_element_type=f32
    )


def eye():
    return (lax.broadcasted_iota(jnp.int32, (R, R), 0) == lax.broadcasted_iota(jnp.int32, (R, R), 1)).astype(f32)


def sum_sq(x):
    return jnp.sum(x * x)


def sweep_inverse(ref):
    lane = lax.broadcasted_iota(jnp.int32, (1, R), 1)
    row_at = lax.broadcasted_iota(jnp.int32, (R, 1), 0)

    def body(k, _):
        a = ref[...]
        row = ref[pl.ds(k, 1), :]
        here = lane == k
        pivot = jnp.sum(jnp.where(here, row, 0.0), axis=1, keepdims=True)
        col = jnp.sum(jnp.where(here, a, 0.0), axis=1, keepdims=True)
        col = jnp.where(row_at == k, 0.0, col)
        row = jnp.where(here, 1.0, row) / pivot
        ref[...] = jnp.where(here, 0.0, a) - col * row
        ref[pl.ds(k, 1), :] = row
        return 0

    lax.fori_loop(0, R, body, 0)


ROWS = 24
INFO = 640


def partials(tm_ref, obs_ref, load_ref, noise_ref, out_ref):
    noise = noise_ref[...]
    column = jnp.broadcast_to(noise, (128, R)).T

    def weighted(i):
        return split(load_ref[:, 128 * i : 128 * i + 128].astype(f32) * column)

    def pairs(i, lo, at):
        rows = load_ref[:, lo:]
        hi, rest = weighted(i)
        blocks = dot1(hi, rows, 0, 0) + dot1(rest, rows, 0, 0)
        for n in range((R - lo) // 128):
            out_ref[at + 128 * n : at + 128 * n + 128, :] = blocks[:, 128 * n : 128 * n + 128]

    def one(i, at):
        rows = load_ref[:, 128 * i : 128 * i + 128]
        hi, rest = weighted(i)
        out_ref[at : at + 128, :] = dot1(hi, rows, 0, 0) + dot1(rest, rows, 0, 0)

    first = lax.rem(tm_ref[0], 2) == 0

    @pl.when(first)
    def _():
        pairs(0, 0, 0)
        one(1, 512)

    @pl.when(jnp.logical_not(first))
    def _():
        pairs(1, 256, 0)
        pairs(2, 256, 256)
        one(3, 512)

    hi, rest = split(obs_ref[...] * noise)
    rows = load_ref[...]
    info = dot1(hi, rows) + dot1(rest, rows)
    for t in range(4):
        for c in range(4):
            out_ref[INFO + 4 * t + c : INFO + 4 * t + c + 1, :] = info[t : t + 1, 128 * c : 128 * c + 128]
    out_ref[INFO + 16 :, :] = jnp.zeros((32 * ROWS - INFO - 16, 128), f32)


def prep_a(dyn_ref, prior_ref, wt_ref, nn_ref, x_ref):
    prior = prior_ref[...]
    psplit = split(prior)
    wt = dot6(dyn_ref[...], prior, 0, 0)
    wt_ref[...] = wt
    nn_ref[...] = dot6(wt, dyn_ref[...])
    col = jnp.sum(jnp.abs(prior), axis=0, keepdims=True)
    start = 1.0 / jnp.max(col, axis=1, keepdims=True)
    ident = eye()
    x = ident * start
    ph = psplit[0]
    x = start * (2.0 * ident - start * prior)
    x_ref[...] = x

    def body(k, _):
        x = x_ref[...]
        xh = x.astype(bf16)
        t = dot1(ph, xh)
        x_ref[...] = 2.0 * x - dot1(xh, t.astype(bf16))
        return 0

    lax.fori_loop(0, 6, body, 0)


def refine(times_mat, x_ref, r_ref, done2, cap, product):
    ident = eye()

    def residual():
        r = ident - times_mat(x_ref[...])
        r_ref[...] = r
        return sum_sq(r)

    def cond(c):
        k, n2, old = c
        return (n2 > done2) & (k < cap) & (n2 < 0.98 * old)

    def body(c):
        k, n2, _ = c
        x = x_ref[...]
        x_ref[...] = x + product(x, r_ref[...])
        return k + 1, residual(), n2

    n0 = residual()
    return lax.while_loop(cond, body, (jnp.int32(0), n0, jnp.float32(jnp.inf)))[1]


def coarse(a, b):
    return dot1(a.astype(bf16), b.astype(bf16))


def fine(a, b):
    return dot3(split(a), split(b))


def prep_b(prior_ref, dyn_ref, x_in, x_ref, rest_ref, wp_ref, r_ref):
    x_ref[...] = x_in[...]
    n2 = refine(lambda v: fine(prior_ref[...], v), x_ref, r_ref, 1e-5, 40, coarse)

    @pl.when(jnp.logical_not(n2 < 1e-3))
    def _():
        x_ref[...] = x_in[...]
        n2 = refine(lambda v: dot6(prior_ref[...], v), x_ref, r_ref, 1e-5, 40, fine)

        @pl.when(jnp.logical_not(n2 < 1e-2))
        def _():
            x_ref[...] = prior_ref[...]
            sweep_inverse(x_ref)

    rest = eye() - dot6(prior_ref[...], x_ref[...])
    rest_ref[...] = rest
    turned = dyn_ref[...].T
    wp_ref[...] = turned - coarse(turned, rest)


PAIRS = ((0, 0), (0, 1), (0, 2), (0, 3), (1, 1), (1, 2), (1, 3), (2, 2), (2, 3), (3, 3))


def copies(sources, targets, sems):
    return [pltpu.make_async_copy(a, b, sems.at[n]) for n, (a, b) in enumerate(zip(sources, targets))]


def invert(tm_ref, *refs):
    sources, results, held, made, (g_ref, r_ref, sems, out_sems) = refs[:8], refs[8:11], refs[11:19], refs[19:22], refs[22:]
    own_ref, other_ref, pinv_ref, rest_ref, wp_ref, prior_ref, nn_ref, wt_ref = held
    x_ref, ft_ref, m_ref = made
    loads = copies(sources, held, sems)
    stores = copies(made, results, out_sems)
    for c in loads:
        c.start()
    loads[0].wait()
    loads[1].wait()
    first = lax.rem(tm_ref[0], 2) == 0
    for n, (i, j) in enumerate(PAIRS):
        at = (n % 5) * 128
        mine, theirs = own_ref[at : at + 128, :], other_ref[at : at + 128, :]
        blk = jnp.where(first, mine, theirs) if n < 5 else jnp.where(first, theirs, mine)
        g_ref[128 * i : 128 * i + 128, 128 * j : 128 * j + 128] = blk
        if i != j:
            g_ref[128 * j : 128 * j + 128, 128 * i : 128 * i + 128] = blk.T
    gram = g_ref[...]
    loads[2].wait()
    loads[3].wait()
    psplit = split(pinv_ref[...])
    h = dot3(split(gram), psplit) - rest_ref[...]
    hs = split(h)
    t = dot1(hs[0], hs[0])
    s = t - h - dot1(hs[0], t.astype(bf16))
    ss = split(s)
    r = -(h + s + dot3(hs, ss))
    n2 = sum_sq(r)
    rh = r.astype(bf16)
    r = r + dot1(rh, rh)
    s = s + r + dot1(ss[0], r.astype(bf16))
    ss = split(s)
    for c in loads[4:]:
        c.wait()
    m_ref[...] = gram + (prior_ref[...] - nn_ref[...])
    stores[2].start()
    wp = wp_ref[...]
    x_ref[...] = pinv_ref[...] + dot3(psplit, ss)
    ft_ref[...] = wp + dot3(split(wp), ss)

    @pl.when(jnp.logical_not(n2 < 1e-4))
    def _():
        e = coarse(g_ref[...], pinv_ref[...])
        theta = 2.0 / (2.0 + jnp.sqrt(sum_sq(e)))
        x_ref[...] = theta * pinv_ref[...]
        n2 = refine(lambda v: dot6(prior_ref[...] + g_ref[...], v), x_ref, r_ref, 1e-9, 60, fine)

        @pl.when(jnp.logical_not(n2 < 1e-6))
        def _():
            x_ref[...] = prior_ref[...] + g_ref[...]
            sweep_inverse(x_ref)

        ft_ref[...] = dot6(wt_ref[...], x_ref[...])

    stores[0].start()
    stores[1].start()
    for c in stores:
        c.wait()


def scans(tm_ref, *refs):
    sources, (filt_ref, smooth_ref), held, (f_ref, s_ref, sems) = refs[:5], refs[5:7], refs[7:12], refs[12:]
    ft_ref, info_ref, x_ref, m_ref, nn_ref = held
    loads = copies(sources, held, sems)
    for c in loads:
        c.start()
    T = 64
    loads[0].wait()
    f = ft_ref[...]
    powers = [split(f)]
    ident = eye()
    c = jnp.sum(jnp.sum(f * ident, axis=0, keepdims=True), axis=1, keepdims=True) * (1.0 / R)
    e = f - c * ident
    es = split(e)
    f = c * (f + e) + dot3(es, es)
    powers.append(split(f))
    loads[1].wait()
    loads[2].wait()
    x = split(x_ref[...])
    parts = [info_ref[pl.ds(c, T, stride=4), :] for c in range(4)]
    info = jnp.concatenate(parts, axis=1)
    y = dot3(split(info), x)
    for _ in range(4):
        f = dot3(powers[-1], powers[-1])
        powers.append(split(f))
    step = lax.broadcasted_iota(jnp.int32, (T, 1), 0)

    def later(v, k):
        return jnp.where(step >= k, pltpu.roll(v, k, 0), 0.0)

    def sooner(v, k):
        return jnp.where(step < T - k, pltpu.roll(v, T - k, 0), 0.0)

    for n, p in enumerate(powers):
        y = y + later(dot3(split(y), p), 1 << n)
    f_ref[...] = y
    loads[3].wait()
    loads[4].wait()
    nn = nn_ref[...]
    ys = split(y)
    u = dot3(ys, split(m_ref[...]))
    tail = dot3(split(y[T - 8 :, :]), split(nn))
    u = u + jnp.where(step == T - 1, jnp.concatenate([jnp.zeros((T - 8, R), f32), tail], axis=0), 0.0)
    for n, p in enumerate(powers):
        u = u + sooner(dot3(split(u), p, 1, 1), 1 << n)
    s_ref[...] = dot3(split(u), x)
    at = pl.multiple_of(8 * lax.div(tm_ref[0], 2), 8)
    half = lax.rem(tm_ref[0], 2) == 0
    fb = f_ref[pl.ds(at, 8), :]
    sb = s_ref[pl.ds(at, 8), :]
    filt_ref[...] = jnp.where(half, fb[0:4], fb[4:8])
    smooth_ref[...] = jnp.where(half, sb[0:4], sb[4:8])


vm = partial(pltpu.VMEM, (R, R), f32)
mat = jax.ShapeDtypeStruct((R, R), f32)
smem = pl.BlockSpec(memory_space=pltpu.SMEM)
vmem = pl.BlockSpec(memory_space=pltpu.VMEM)
room = pltpu.CompilerParams(vmem_limit_bytes=28 << 20)


anywhere = pl.BlockSpec(memory_space=pl.ANY)
far = pltpu.HBM((R, R), f32)


def kept_far(arrays):
    return [pltpu.with_memory_space_constraint(a, pltpu.HBM) for a in arrays]

part = pltpu.VMEM((32 * ROWS, 128), f32)


def prep_first(dyn, prior):
    return pl.pallas_call(prep_a, out_shape=(mat, mat, mat), name="prep_a")(dyn, prior)


def prep_second(prior, dyn, x):
    return pl.pallas_call(prep_b, out_shape=(mat, mat, mat), scratch_shapes=[vm()], name="prep_b")(prior, dyn, x)


def inverse(tm, *arrays):
    dma = pltpu.SemaphoreType.DMA
    return pl.pallas_call(
        invert,
        out_shape=(far, far, far),
        in_specs=[smem] + [anywhere] * 8,
        out_specs=(anywhere,) * 3,
        scratch_shapes=[part, part] + [vm()] * 11 + [dma((8,)), dma((3,))],
        name="invert",
        compiler_params=room,
    )(tm, *arrays[:2], *kept_far(arrays[2:]))


def time_scans(tm, *arrays):
    out = jax.ShapeDtypeStruct((4, R), f32)
    rows = pltpu.VMEM((64, R), f32)
    return pl.pallas_call(
        scans,
        out_shape=(out, out),
        in_specs=[smem] + [anywhere] * 5,
        scratch_shapes=[vm(), pltpu.VMEM((256, 128), f32), vm(), vm(), vm(), rows, rows, pltpu.SemaphoreType.DMA((5,))],
        name="scans",
        compiler_params=room,
    )(tm, *kept_far(arrays[:1]), arrays[1], *kept_far(arrays[2:]))


def local_partials(tm, observed, loadings, noise):
    return pl.pallas_call(
        partials,
        out_shape=jax.ShapeDtypeStruct((32 * ROWS, 128), f32),
        in_specs=[smem] + [vmem] * 3,
        name="partials",
    )(tm, observed, loadings, noise)


def exchange(pieces, axis):
    return lax.all_to_all(pieces, axis, split_axis=0, concat_axis=0, tiled=True)


def shards(observed, loadings, noise_prec, dynamics, prior_prec):
    tm = lax.axis_index("tm").astype(jnp.int32).reshape(1)
    send = local_partials(tm, observed, loadings, noise_prec.reshape(1, R))
    send, dynamics, prior_prec = lax.optimization_barrier((send, dynamics, prior_prec))
    pieces = exchange(send.reshape(32, ROWS, 128), "sens")
    wt, nn, x0 = prep_first(dynamics, prior_prec)
    total = jnp.broadcast_to(pieces.sum(axis=0), pieces.shape)
    total, x0 = lax.optimization_barrier((total, x0))
    own = exchange(total, "sens").reshape(32 * ROWS, 128)
    pinv, rest, wp = prep_second(prior_prec, dynamics, x0)
    own, pinv = lax.optimization_barrier((own, pinv))
    other = lax.ppermute(own, "tm", [(i, i ^ 1) for i in range(16)])
    info = jnp.broadcast_to(own[INFO : INFO + 16], (16, 16, 128))
    info = exchange(info, "tm").reshape(256, 128)
    x, ft, m = inverse(tm, own, other, pinv, rest, wp, prior_prec, nn, wt)
    return time_scans(tm, ft, info, x, m, nn)


def solution(mesh):
    return jax.shard_map(
        shards,
        mesh=mesh,
        in_specs=(P("tm", "sens"), P("sens", None), P("sens"), P(), P()),
        out_specs=(P("tm", None), P("tm", None)),
        check_vma=False,
    )
```

```python
from functools import partial

import jax
import jax.numpy as jnp
from jax import lax
from jax.experimental import pallas as pl
from jax.experimental.pallas import tpu as pltpu
from jax.sharding import PartitionSpec as P

f32 = jnp.float32
bf16 = jnp.bfloat16
R = 512


def dot1(a, b, ca=1, cb=0):
    return lax.dot_general(a, b, (((ca,), (cb,)), ((), ())), preferred_element_type=f32)


def split(a):
    hi = a.astype(bf16)
    return hi, (a - hi.astype(f32)).astype(bf16)


def dot3(a, b, ca=1, cb=0):
    return dot1(a[0], b[0], ca, cb) + (dot1(a[0], b[1], ca, cb) + dot1(a[1], b[0], ca, cb))


def rows3(a, b, ca=1, cb=0):
    n = a[0].shape[0]
    both = dot1(jnp.concatenate(a, axis=0), b[0], ca, cb)
    return both[:n] + (both[n:] + dot1(a[0], b[1], ca, cb))


def dot6(a, b, ca=1, cb=0):
    return lax.dot_general(
        a, b, (((ca,), (cb,)), ((), ())), precision=lax.Precision.HIGHEST, preferred_element_type=f32
    )


def eye():
    return (lax.broadcasted_iota(jnp.int32, (R, R), 0) == lax.broadcasted_iota(jnp.int32, (R, R), 1)).astype(f32)


def sum_sq(x):
    return jnp.sum(x * x)


def sweep_inverse(ref):
    lane = lax.broadcasted_iota(jnp.int32, (1, R), 1)
    row_at = lax.broadcasted_iota(jnp.int32, (R, 1), 0)

    def body(k, _):
        a = ref[...]
        row = ref[pl.ds(k, 1), :]
        here = lane == k
        pivot = jnp.sum(jnp.where(here, row, 0.0), axis=1, keepdims=True)
        col = jnp.sum(jnp.where(here, a, 0.0), axis=1, keepdims=True)
        col = jnp.where(row_at == k, 0.0, col)
        row = jnp.where(here, 1.0, row) / pivot
        ref[...] = jnp.where(here, 0.0, a) - col * row
        ref[pl.ds(k, 1), :] = row
        return 0

    lax.fori_loop(0, R, body, 0)


ROWS = 24
INFO = 640


def partials(tm_ref, obs_ref, load_ref, noise_ref, out_ref):
    noise = noise_ref[...]
    column = jnp.broadcast_to(noise, (128, R)).T

    def weighted(i):
        return split(load_ref[:, 128 * i : 128 * i + 128].astype(f32) * column)

    def pairs(i, lo, at):
        rows = load_ref[:, lo:]
        hi, rest = weighted(i)
        blocks = dot1(hi, rows, 0, 0) + dot1(rest, rows, 0, 0)
        for n in range((R - lo) // 128):
            out_ref[at + 128 * n : at + 128 * n + 128, :] = blocks[:, 128 * n : 128 * n + 128]

    def one(i, at):
        rows = load_ref[:, 128 * i : 128 * i + 128]
        hi, rest = weighted(i)
        out_ref[at : at + 128, :] = dot1(hi, rows, 0, 0) + dot1(rest, rows, 0, 0)

    first = lax.rem(tm_ref[0], 2) == 0

    @pl.when(first)
    def _():
        pairs(0, 0, 0)
        one(1, 512)

    @pl.when(jnp.logical_not(first))
    def _():
        pairs(1, 256, 0)
        pairs(2, 256, 256)
        one(3, 512)

    hi, rest = split(obs_ref[...] * noise)
    rows = load_ref[...]
    info = dot1(hi, rows) + dot1(rest, rows)
    for t in range(4):
        for c in range(4):
            out_ref[INFO + 4 * t + c : INFO + 4 * t + c + 1, :] = info[t : t + 1, 128 * c : 128 * c + 128]
    out_ref[INFO + 16 :, :] = jnp.zeros((32 * ROWS - INFO - 16, 128), f32)


def prep_a(dyn_ref, prior_ref, wt_ref, nn_ref, q_ref, x_ref):
    prior = prior_ref[...]
    psplit = split(prior)
    wt = dot6(dyn_ref[...], prior, 0, 0)
    wt_ref[...] = wt
    nn = dot6(wt, dyn_ref[...])
    nn_ref[...] = nn
    q_ref[...] = prior - nn
    col = jnp.sum(jnp.abs(prior), axis=0, keepdims=True)
    start = 1.0 / jnp.max(col, axis=1, keepdims=True)
    ident = eye()
    x = ident * start
    ph = psplit[0]
    x = start * (2.0 * ident - start * prior)
    x_ref[...] = x

    def body(k, _):
        x = x_ref[...]
        xh = x.astype(bf16)
        t = dot1(ph, xh)
        x_ref[...] = 2.0 * x - dot1(xh, t.astype(bf16))
        return 0

    lax.fori_loop(0, 6, body, 0)


def refine(times_mat, x_ref, r_ref, done2, cap, product):
    ident = eye()

    def residual():
        r = ident - times_mat(x_ref[...])
        r_ref[...] = r
        return sum_sq(r)

    def cond(c):
        k, n2, old = c
        return (n2 > done2) & (k < cap) & (n2 < 0.98 * old)

    def body(c):
        k, n2, _ = c
        x = x_ref[...]
        x_ref[...] = x + product(x, r_ref[...])
        return k + 1, residual(), n2

    n0 = residual()
    return lax.while_loop(cond, body, (jnp.int32(0), n0, jnp.float32(jnp.inf)))[1]


def coarse(a, b):
    return dot1(a.astype(bf16), b.astype(bf16))


def fine(a, b):
    return dot3(split(a), split(b))


def prep_b(prior_ref, dyn_ref, x_in, x_ref, rest_ref, wp_ref, r_ref):
    x_ref[...] = x_in[...]
    n2 = refine(lambda v: fine(prior_ref[...], v), x_ref, r_ref, 1e-5, 40, coarse)

    @pl.when(jnp.logical_not(n2 < 1e-3))
    def _():
        x_ref[...] = x_in[...]
        n2 = refine(lambda v: dot6(prior_ref[...], v), x_ref, r_ref, 1e-5, 40, fine)

        @pl.when(jnp.logical_not(n2 < 1e-2))
        def _():
            x_ref[...] = prior_ref[...]
            sweep_inverse(x_ref)

    rest = eye() - dot6(prior_ref[...], x_ref[...])
    rest_ref[...] = rest.astype(bf16)
    turned = dyn_ref[...].T
    wp_ref[...] = turned - coarse(turned, rest)


PAIRS = ((0, 0), (0, 1), (0, 2), (0, 3), (1, 1), (1, 2), (1, 3), (2, 2), (2, 3), (3, 3))


def copies(sources, targets, sems):
    return [pltpu.make_async_copy(a, b, sems.at[n]) for n, (a, b) in enumerate(zip(sources, targets))]


def invert(tm_ref, *refs):
    sources, results, held, made, (g_ref, r_ref, sems, out_sems) = refs[:8], refs[8:11], refs[11:19], refs[19:22], refs[22:]
    own_ref, other_ref, pinv_ref, rest_ref, wp_ref, q_ref, prior_ref, wt_ref = held
    x_ref, ft_ref, m_ref = made
    loads = copies(sources, held, sems)
    stores = copies(made, results, out_sems)
    for c in loads[:4]:
        c.start()
    loads[0].wait()
    loads[1].wait()
    first = lax.rem(tm_ref[0], 2) == 0
    for n, (i, j) in enumerate(PAIRS):
        at = (n % 5) * 128
        mine, theirs = own_ref[at : at + 128, :], other_ref[at : at + 128, :]
        blk = jnp.where(first, mine, theirs) if n < 5 else jnp.where(first, theirs, mine)
        g_ref[128 * i : 128 * i + 128, 128 * j : 128 * j + 128] = blk
        if i != j:
            g_ref[128 * j : 128 * j + 128, 128 * i : 128 * i + 128] = blk.T
    gram = g_ref[...]
    loads[2].wait()
    loads[3].wait()
    loads[4].start()
    loads[5].start()
    psplit = split(pinv_ref[...])
    h = dot3(split(gram), psplit) - rest_ref[...].astype(f32)
    h0, h1 = split(h)
    r = (h0.astype(f32) - h) + (dot1(h0, h0) + dot1(h1, h0))
    rh = r.astype(bf16)
    rr = dot1(rh, rh)
    n4 = sum_sq(rr)
    r = r + rr + dot1(rh, rr.astype(bf16))
    s = r - h0.astype(f32) - dot1(h0, r.astype(bf16))
    ss = split(s)
    loads[4].wait()
    loads[5].wait()
    m_ref[...] = gram + q_ref[...]
    stores[2].start()
    wp = wp_ref[...]
    good = n4 < 1e-6

    @pl.when(good)
    def _():
        x_ref[...] = pinv_ref[...] + dot3(psplit, ss)
        stores[0].start()
        ft_ref[...] = wp + dot3(split(wp), ss)
        stores[1].start()

    @pl.when(jnp.logical_not(good))
    def _():
        for c in loads[6:]:
            c.start()
            c.wait()
        e = coarse(g_ref[...], pinv_ref[...])
        theta = 2.0 / (2.0 + jnp.sqrt(sum_sq(e)))
        x_ref[...] = theta * pinv_ref[...]
        n2 = refine(lambda v: dot6(prior_ref[...] + g_ref[...], v), x_ref, r_ref, 1e-9, 60, fine)

        @pl.when(jnp.logical_not(n2 < 1e-6))
        def _():
            x_ref[...] = prior_ref[...] + g_ref[...]
            sweep_inverse(x_ref)

        ft_ref[...] = dot6(wt_ref[...], x_ref[...])
        stores[0].start()
        stores[1].start()

    for c in stores:
        c.wait()


def scans(tm_ref, *refs):
    sources, (filt_ref, smooth_ref), held, (f_ref, s_ref, sems) = refs[:5], refs[5:7], refs[7:12], refs[12:]
    ft_ref, info_ref, x_ref, m_ref, nn_ref = held
    loads = copies(sources, held, sems)
    for c in loads:
        c.start()
    T = 64
    loads[0].wait()
    f = ft_ref[...]
    powers = [split(f)]
    ident = eye()
    c = jnp.sum(jnp.sum(f * ident, axis=0, keepdims=True), axis=1, keepdims=True) * (1.0 / R)
    e = f - c * ident
    es = split(e)
    f = c * (f + e) + dot3(es, es)
    powers.append(split(f))
    loads[1].wait()
    loads[2].wait()
    x = split(x_ref[...])
    parts = [info_ref[pl.ds(c, T, stride=4), :] for c in range(4)]
    info = jnp.concatenate(parts, axis=1)
    y = rows3(split(info), x)
    for _ in range(3):
        f = dot3(powers[-1], powers[-1])
        powers.append(split(f))
    leap = powers.pop()
    step = lax.broadcasted_iota(jnp.int32, (T, 1), 0)

    def later(v, k):
        return jnp.where(step >= k, pltpu.roll(v, k, 0), 0.0)

    def sooner(v, k):
        return jnp.where(step < T - k, pltpu.roll(v, T - k, 0), 0.0)

    for n, p in enumerate(powers):
        y = y + later(rows3(split(y), p), 1 << n)
    blocks = [y[16 * b : 16 * b + 16] for b in range(4)]
    for b in range(1, 4):
        blocks[b] = blocks[b] + rows3(split(blocks[b - 1]), leap)
    y = jnp.concatenate(blocks, axis=0)
    f_ref[...] = y
    loads[3].wait()
    loads[4].wait()
    nn = nn_ref[...]
    ys = split(y)
    u = rows3(ys, split(m_ref[...]))
    tail = dot3(split(y[T - 8 :, :]), split(nn))
    u = u + jnp.where(step == T - 1, jnp.concatenate([jnp.zeros((T - 8, R), f32), tail], axis=0), 0.0)
    for n, p in enumerate(powers):
        u = u + sooner(rows3(split(u), p, 1, 1), 1 << n)
    blocks = [u[16 * b : 16 * b + 16] for b in range(4)]
    for b in range(2, -1, -1):
        blocks[b] = blocks[b] + rows3(split(blocks[b + 1]), leap, 1, 1)
    u = jnp.concatenate(blocks, axis=0)
    s_ref[...] = rows3(split(u), x)
    at = pl.multiple_of(8 * lax.div(tm_ref[0], 2), 8)
    half = lax.rem(tm_ref[0], 2) == 0
    fb = f_ref[pl.ds(at, 8), :]
    sb = s_ref[pl.ds(at, 8), :]
    filt_ref[...] = jnp.where(half, fb[0:4], fb[4:8])
    smooth_ref[...] = jnp.where(half, sb[0:4], sb[4:8])


vm = partial(pltpu.VMEM, (R, R), f32)
mat = jax.ShapeDtypeStruct((R, R), f32)
half = jax.ShapeDtypeStruct((R, R), bf16)
smem = pl.BlockSpec(memory_space=pltpu.SMEM)
vmem = pl.BlockSpec(memory_space=pltpu.VMEM)
room = pltpu.CompilerParams(vmem_limit_bytes=28 << 20)


anywhere = pl.BlockSpec(memory_space=pl.ANY)
far = pltpu.HBM((R, R), f32)


def kept_far(arrays):
    return [pltpu.with_memory_space_constraint(a, pltpu.HBM) for a in arrays]

part = pltpu.VMEM((32 * ROWS, 128), f32)


def prep_first(dyn, prior):
    return pl.pallas_call(prep_a, out_shape=(mat,) * 4, name="prep_a")(dyn, prior)


def prep_second(prior, dyn, x):
    return pl.pallas_call(prep_b, out_shape=(mat, half, mat), scratch_shapes=[vm()], name="prep_b")(prior, dyn, x)


def inverse(tm, *arrays):
    dma = pltpu.SemaphoreType.DMA
    return pl.pallas_call(
        invert,
        out_shape=(far, far, far),
        in_specs=[smem] + [anywhere] * 8,
        out_specs=(anywhere,) * 3,
        scratch_shapes=[part, part, vm(), pltpu.VMEM((R, R), bf16)] + [vm()] * 9 + [dma((8,)), dma((3,))],
        name="invert",
        compiler_params=room,
    )(tm, *arrays[:2], *kept_far(arrays[2:]))


def time_scans(tm, *arrays):
    out = jax.ShapeDtypeStruct((4, R), f32)
    rows = pltpu.VMEM((64, R), f32)
    return pl.pallas_call(
        scans,
        out_shape=(out, out),
        in_specs=[smem] + [anywhere] * 5,
        scratch_shapes=[vm(), pltpu.VMEM((256, 128), f32), vm(), vm(), vm(), rows, rows, pltpu.SemaphoreType.DMA((5,))],
        name="scans",
        compiler_params=room,
    )(tm, *kept_far(arrays[:1]), arrays[1], *kept_far(arrays[2:]))


def local_partials(tm, observed, loadings, noise):
    return pl.pallas_call(
        partials,
        out_shape=jax.ShapeDtypeStruct((32 * ROWS, 128), f32),
        in_specs=[smem] + [vmem] * 3,
        name="partials",
    )(tm, observed, loadings, noise)


def exchange(pieces, axis):
    return lax.all_to_all(pieces, axis, split_axis=0, concat_axis=0, tiled=True)


def shards(observed, loadings, noise_prec, dynamics, prior_prec):
    tm = lax.axis_index("tm").astype(jnp.int32).reshape(1)
    send = local_partials(tm, observed, loadings, noise_prec.reshape(1, R))
    send, dynamics, prior_prec = lax.optimization_barrier((send, dynamics, prior_prec))
    pieces = exchange(send.reshape(32, ROWS, 128), "sens")
    wt, nn, q, x0 = prep_first(dynamics, prior_prec)
    total = jnp.broadcast_to(pieces.sum(axis=0), pieces.shape)
    total, x0 = lax.optimization_barrier((total, x0))
    own = exchange(total, "sens").reshape(32 * ROWS, 128)
    pinv, rest, wp = prep_second(prior_prec, dynamics, x0)
    own, pinv = lax.optimization_barrier((own, pinv))
    other = lax.ppermute(own, "tm", [(i, i ^ 1) for i in range(16)])
    info = jnp.broadcast_to(own[INFO : INFO + 16], (16, 16, 128))
    info = exchange(info, "tm").reshape(256, 128)
    x, ft, m = inverse(tm, own, other, pinv, rest, wp, q, prior_prec, wt)
    return time_scans(tm, ft, info, x, m, nn)


def solution(mesh):
    return jax.shard_map(
        shards,
        mesh=mesh,
        in_specs=(P("tm", "sens"), P("sens", None), P("sens"), P(), P()),
        out_specs=(P("tm", None), P("tm", None)),
        check_vma=False,
    )
```

```python
from functools import partial

import jax
import jax.numpy as jnp
from jax import lax
from jax.experimental import pallas as pl
from jax.experimental.pallas import tpu as pltpu
from jax.sharding import PartitionSpec as P

f32 = jnp.float32
bf16 = jnp.bfloat16
R = 512


def dot1(a, b, ca=1, cb=0):
    return lax.dot_general(a, b, (((ca,), (cb,)), ((), ())), preferred_element_type=f32)


def split(a):
    hi = a.astype(bf16)
    return hi, (a - hi.astype(f32)).astype(bf16)


def dot3(a, b, ca=1, cb=0):
    return dot1(a[0], b[0], ca, cb) + (dot1(a[0], b[1], ca, cb) + dot1(a[1], b[0], ca, cb))


def rows3(a, b, ca=1, cb=0):
    n = a[0].shape[0]
    both = dot1(jnp.concatenate(a, axis=0), b[0], ca, cb)
    return both[:n] + (both[n:] + dot1(a[0], b[1], ca, cb))


def dot6(a, b, ca=1, cb=0):
    return lax.dot_general(
        a, b, (((ca,), (cb,)), ((), ())), precision=lax.Precision.HIGHEST, preferred_element_type=f32
    )


def eye():
    return (lax.broadcasted_iota(jnp.int32, (R, R), 0) == lax.broadcasted_iota(jnp.int32, (R, R), 1)).astype(f32)


def sum_sq(x):
    return jnp.sum(x * x)


def sweep_inverse(ref):
    lane = lax.broadcasted_iota(jnp.int32, (1, R), 1)
    row_at = lax.broadcasted_iota(jnp.int32, (R, 1), 0)

    def body(k, _):
        a = ref[...]
        row = ref[pl.ds(k, 1), :]
        here = lane == k
        pivot = jnp.sum(jnp.where(here, row, 0.0), axis=1, keepdims=True)
        col = jnp.sum(jnp.where(here, a, 0.0), axis=1, keepdims=True)
        col = jnp.where(row_at == k, 0.0, col)
        row = jnp.where(here, 1.0, row) / pivot
        ref[...] = jnp.where(here, 0.0, a) - col * row
        ref[pl.ds(k, 1), :] = row
        return 0

    lax.fori_loop(0, R, body, 0)


ROWS = 24
INFO = 640


def partials(tm_ref, obs_ref, load_ref, noise_ref, out_ref):
    noise = noise_ref[...]
    column = jnp.broadcast_to(noise, (128, R)).T

    def weighted(i):
        return split(load_ref[:, 128 * i : 128 * i + 128].astype(f32) * column)

    def pairs(i, lo, at):
        rows = load_ref[:, lo:]
        hi, rest = weighted(i)
        blocks = dot1(hi, rows, 0, 0) + dot1(rest, rows, 0, 0)
        for n in range((R - lo) // 128):
            out_ref[at + 128 * n : at + 128 * n + 128, :] = blocks[:, 128 * n : 128 * n + 128]

    def one(i, at):
        rows = load_ref[:, 128 * i : 128 * i + 128]
        hi, rest = weighted(i)
        out_ref[at : at + 128, :] = dot1(hi, rows, 0, 0) + dot1(rest, rows, 0, 0)

    first = lax.rem(tm_ref[0], 2) == 0

    @pl.when(first)
    def _():
        pairs(0, 0, 0)
        one(1, 512)

    @pl.when(jnp.logical_not(first))
    def _():
        pairs(1, 256, 0)
        pairs(2, 256, 256)
        one(3, 512)

    hi, rest = split(obs_ref[...] * noise)
    rows = load_ref[...]
    info = dot1(hi, rows) + dot1(rest, rows)
    for t in range(4):
        for c in range(4):
            out_ref[INFO + 4 * t + c : INFO + 4 * t + c + 1, :] = info[t : t + 1, 128 * c : 128 * c + 128]
    out_ref[INFO + 16 :, :] = jnp.zeros((32 * ROWS - INFO - 16, 128), f32)


def prep_a(dyn_ref, prior_ref, wt_ref, nn_ref, q_ref, x_ref):
    prior = prior_ref[...]
    psplit = split(prior)
    wt = dot6(dyn_ref[...], prior, 0, 0)
    wt_ref[...] = wt
    nn = dot6(wt, dyn_ref[...])
    nn_ref[...] = nn
    q_ref[...] = prior - nn
    col = jnp.sum(jnp.abs(prior), axis=0, keepdims=True)
    start = 1.0 / jnp.max(col, axis=1, keepdims=True)
    ident = eye()
    x = ident * start
    ph = psplit[0]
    x = start * (2.0 * ident - start * prior)
    x_ref[...] = x

    def body(k, _):
        x = x_ref[...]
        xh = x.astype(bf16)
        t = dot1(ph, xh)
        x_ref[...] = 2.0 * x - dot1(xh, t.astype(bf16))
        return 0

    lax.fori_loop(0, 6, body, 0)


def refine(times_mat, x_ref, r_ref, done2, cap, product):
    ident = eye()

    def residual():
        r = ident - times_mat(x_ref[...])
        r_ref[...] = r
        return sum_sq(r)

    def cond(c):
        k, n2, old = c
        return (n2 > done2) & (k < cap) & (n2 < 0.98 * old)

    def body(c):
        k, n2, _ = c
        x = x_ref[...]
        x_ref[...] = x + product(x, r_ref[...])
        return k + 1, residual(), n2

    n0 = residual()
    return lax.while_loop(cond, body, (jnp.int32(0), n0, jnp.float32(jnp.inf)))[1]


def coarse(a, b):
    return dot1(a.astype(bf16), b.astype(bf16))


def fine(a, b):
    return dot3(split(a), split(b))


def prep_b(prior_ref, dyn_ref, x_in, x_ref, rest_ref, wp_ref, c_ref, r_ref):
    x_ref[...] = x_in[...]
    n2 = refine(lambda v: fine(prior_ref[...], v), x_ref, r_ref, 1e-5, 40, coarse)

    @pl.when(jnp.logical_not(n2 < 1e-3))
    def _():
        x_ref[...] = x_in[...]
        n2 = refine(lambda v: dot6(prior_ref[...], v), x_ref, r_ref, 1e-5, 40, fine)

        @pl.when(jnp.logical_not(n2 < 1e-2))
        def _():
            x_ref[...] = prior_ref[...]
            sweep_inverse(x_ref)

    rest = eye() - dot6(prior_ref[...], x_ref[...])
    rest_ref[...] = rest.astype(bf16)
    turned = dyn_ref[...].T
    wp_ref[...] = turned - coarse(turned, rest)
    mean = jnp.sum(jnp.sum(turned * eye(), axis=0, keepdims=True), axis=1, keepdims=True) * (1.0 / R)
    c_ref[...] = jnp.broadcast_to(mean, (8, 128))


PAIRS = ((0, 0), (0, 1), (0, 2), (0, 3), (1, 1), (1, 2), (1, 3), (2, 2), (2, 3), (3, 3))


def copies(sources, targets, sems):
    return [pltpu.make_async_copy(a, b, sems.at[n]) for n, (a, b) in enumerate(zip(sources, targets))]


def invert(tm_ref, *refs):
    sources, results, held, made, (g_ref, r_ref, sems, out_sems) = refs[2:8], refs[8:11], refs[11:17], refs[17:20], refs[20:]
    own_ref, other_ref = refs[:2]
    pinv_ref, rest_ref, wp_ref, q_ref, prior_ref, wt_ref = held
    x_ref, ft_ref, m_ref = made
    loads = copies(sources, held, sems)
    stores = copies(made, results, out_sems)
    for c in loads[:4]:
        c.start()
    first = lax.rem(tm_ref[0], 2) == 0
    for n, (i, j) in enumerate(PAIRS):
        at = (n % 5) * 128
        mine, theirs = own_ref[at : at + 128, :], other_ref[at : at + 128, :]
        blk = jnp.where(first, mine, theirs) if n < 5 else jnp.where(first, theirs, mine)
        g_ref[128 * i : 128 * i + 128, 128 * j : 128 * j + 128] = blk
        if i != j:
            g_ref[128 * j : 128 * j + 128, 128 * i : 128 * i + 128] = blk.T
    gram = g_ref[...]
    loads[0].wait()
    loads[1].wait()
    psplit = split(pinv_ref[...])
    h = dot3(split(gram), psplit) - rest_ref[...].astype(f32)
    h0, h1 = split(h)
    r = (h0.astype(f32) - h) + (dot1(h0, h0) + dot1(h1, h0))
    rh = r.astype(bf16)
    rr = dot1(rh, rh)
    n4 = sum_sq(rr)
    r = r + rr + dot1(rh, rr.astype(bf16))
    s = r - h0.astype(f32) - dot1(h0, r.astype(bf16))
    ss = split(s)
    loads[2].wait()
    loads[3].wait()
    m_ref[...] = gram + q_ref[...]
    stores[2].start()
    wp = wp_ref[...]
    good = n4 < 1e-6

    @pl.when(good)
    def _():
        x_ref[...] = pinv_ref[...] + dot3(psplit, ss)
        stores[0].start()
        ft_ref[...] = wp + dot3(split(wp), ss)
        stores[1].start()

    @pl.when(jnp.logical_not(good))
    def _():
        for c in loads[4:]:
            c.start()
            c.wait()
        e = coarse(g_ref[...], pinv_ref[...])
        theta = 2.0 / (2.0 + jnp.sqrt(sum_sq(e)))
        x_ref[...] = theta * pinv_ref[...]
        n2 = refine(lambda v: dot6(prior_ref[...] + g_ref[...], v), x_ref, r_ref, 1e-9, 60, fine)

        @pl.when(jnp.logical_not(n2 < 1e-6))
        def _():
            x_ref[...] = prior_ref[...] + g_ref[...]
            sweep_inverse(x_ref)

        ft_ref[...] = dot6(wt_ref[...], x_ref[...])
        stores[0].start()
        stores[1].start()

    for c in stores:
        c.wait()


def scans(tm_ref, *refs):
    sources, (filt_ref, smooth_ref), held, (f_ref, s_ref, sems) = refs[:6], refs[6:8], refs[8:14], refs[14:]
    ft_ref, info_ref, x_ref, m_ref, nn_ref, c_ref = held
    loads = copies(sources, held, sems)
    for c in loads:
        c.start()
    T = 64
    loads[0].wait()
    loads[5].wait()
    f = ft_ref[...]
    powers = [split(f)]
    c = c_ref[0:1, 0:1]
    e = f - c * eye()
    es = split(e)
    f = c * (f + e) + dot3(es, es)
    powers.append(split(f))
    loads[1].wait()
    loads[2].wait()
    x = split(x_ref[...])
    parts = [info_ref[pl.ds(c, T, stride=4), :] for c in range(4)]
    info = jnp.concatenate(parts, axis=1)
    y = rows3(split(info), x)
    for _ in range(3):
        f = dot3(powers[-1], powers[-1])
        powers.append(split(f))
    leap = powers.pop()
    step = lax.broadcasted_iota(jnp.int32, (T, 1), 0)

    def later(v, k):
        return jnp.where(step >= k, pltpu.roll(v, k, 0), 0.0)

    def sooner(v, k):
        return jnp.where(step < T - k, pltpu.roll(v, T - k, 0), 0.0)

    for n, p in enumerate(powers):
        y = y + later(rows3(split(y), p), 1 << n)
    blocks = [y[16 * b : 16 * b + 16] for b in range(4)]
    for b in range(1, 4):
        blocks[b] = blocks[b] + rows3(split(blocks[b - 1]), leap)
    y = jnp.concatenate(blocks, axis=0)
    f_ref[...] = y
    loads[3].wait()
    loads[4].wait()
    nn = nn_ref[...]
    ys = split(y)
    u = rows3(ys, split(m_ref[...]))
    tail = dot3(split(y[T - 8 :, :]), split(nn))
    u = u + jnp.where(step == T - 1, jnp.concatenate([jnp.zeros((T - 8, R), f32), tail], axis=0), 0.0)
    for n, p in enumerate(powers):
        u = u + sooner(rows3(split(u), p, 1, 1), 1 << n)
    blocks = [u[16 * b : 16 * b + 16] for b in range(4)]
    for b in range(2, -1, -1):
        blocks[b] = blocks[b] + rows3(split(blocks[b + 1]), leap, 1, 1)
    u = jnp.concatenate(blocks, axis=0)
    s_ref[...] = rows3(split(u), x)
    at = pl.multiple_of(8 * lax.div(tm_ref[0], 2), 8)
    half = lax.rem(tm_ref[0], 2) == 0
    fb = f_ref[pl.ds(at, 8), :]
    sb = s_ref[pl.ds(at, 8), :]
    filt_ref[...] = jnp.where(half, fb[0:4], fb[4:8])
    smooth_ref[...] = jnp.where(half, sb[0:4], sb[4:8])


vm = partial(pltpu.VMEM, (R, R), f32)
mat = jax.ShapeDtypeStruct((R, R), f32)
half = jax.ShapeDtypeStruct((R, R), bf16)
tile = jax.ShapeDtypeStruct((8, 128), f32)
smem = pl.BlockSpec(memory_space=pltpu.SMEM)
vmem = pl.BlockSpec(memory_space=pltpu.VMEM)
room = pltpu.CompilerParams(vmem_limit_bytes=28 << 20)


anywhere = pl.BlockSpec(memory_space=pl.ANY)
far = pltpu.HBM((R, R), f32)


def near(arrays):
    return [pltpu.with_memory_space_constraint(a, pltpu.VMEM) for a in arrays]


def kept_far(arrays):
    return [pltpu.with_memory_space_constraint(a, pltpu.HBM) for a in arrays]

part = pltpu.VMEM((32 * ROWS, 128), f32)


def prep_first(dyn, prior):
    return pl.pallas_call(prep_a, out_shape=(mat,) * 4, name="prep_a")(dyn, prior)


def prep_second(prior, dyn, x):
    return pl.pallas_call(prep_b, out_shape=(mat, half, mat, tile), scratch_shapes=[vm()], name="prep_b")(prior, dyn, x)


def inverse(tm, *arrays):
    dma = pltpu.SemaphoreType.DMA
    return pl.pallas_call(
        invert,
        out_shape=(far, far, far),
        in_specs=[smem] + [vmem] * 2 + [anywhere] * 6,
        out_specs=(anywhere,) * 3,
        scratch_shapes=[vm(), pltpu.VMEM((R, R), bf16)] + [vm()] * 9 + [dma((6,)), dma((3,))],
        name="invert",
        compiler_params=room,
    )(tm, *near(arrays[:2]), *kept_far(arrays[2:]))


def time_scans(tm, *arrays):
    out = jax.ShapeDtypeStruct((4, R), f32)
    rows = pltpu.VMEM((64, R), f32)
    return pl.pallas_call(
        scans,
        out_shape=(out, out),
        in_specs=[smem] + [anywhere] * 6,
        scratch_shapes=[vm(), pltpu.VMEM((256, 128), f32), vm(), vm(), vm(), pltpu.VMEM((8, 128), f32), rows, rows, pltpu.SemaphoreType.DMA((6,))],
        name="scans",
        compiler_params=room,
    )(tm, *kept_far(arrays[:1]), arrays[1], *kept_far(arrays[2:]))


def local_partials(tm, observed, loadings, noise):
    return pl.pallas_call(
        partials,
        out_shape=jax.ShapeDtypeStruct((32 * ROWS, 128), f32),
        in_specs=[smem] + [vmem] * 3,
        name="partials",
    )(tm, observed, loadings, noise)


def exchange(pieces, axis):
    return lax.all_to_all(pieces, axis, split_axis=0, concat_axis=0, tiled=True)


def shards(observed, loadings, noise_prec, dynamics, prior_prec):
    tm = lax.axis_index("tm").astype(jnp.int32).reshape(1)
    send = local_partials(tm, observed, loadings, noise_prec.reshape(1, R))
    send, dynamics, prior_prec = lax.optimization_barrier((send, dynamics, prior_prec))
    pieces = exchange(send.reshape(32, ROWS, 128), "sens")
    wt, nn, q, x0 = prep_first(dynamics, prior_prec)
    total = jnp.broadcast_to(pieces.sum(axis=0), pieces.shape)
    total, x0 = lax.optimization_barrier((total, x0))
    own = exchange(total, "sens").reshape(32 * ROWS, 128)
    pinv, rest, wp, c = prep_second(prior_prec, dynamics, x0)
    own, pinv = lax.optimization_barrier((own, pinv))
    other = lax.ppermute(own, "tm", [(i, i ^ 1) for i in range(16)])
    info = jnp.broadcast_to(own[INFO : INFO + 16], (16, 16, 128))
    info = exchange(info, "tm").reshape(256, 128)
    x, ft, m = inverse(tm, own, other, pinv, rest, wp, q, prior_prec, wt)
    return time_scans(tm, ft, info, x, m, nn, c)


def solution(mesh):
    return jax.shard_map(
        shards,
        mesh=mesh,
        in_specs=(P("tm", "sens"), P("sens", None), P("sens"), P(), P()),
        out_specs=(P("tm", None), P("tm", None)),
        check_vma=False,
    )
```

```python
from functools import partial

import jax
import jax.numpy as jnp
from jax import lax
from jax.experimental import pallas as pl
from jax.experimental.pallas import tpu as pltpu
from jax.sharding import PartitionSpec as P

f32 = jnp.float32
bf16 = jnp.bfloat16
R = 512


def dot1(a, b, ca=1, cb=0):
    return lax.dot_general(a, b, (((ca,), (cb,)), ((), ())), preferred_element_type=f32)


def split(a):
    hi = a.astype(bf16)
    return hi, (a - hi.astype(f32)).astype(bf16)


def dot3(a, b, ca=1, cb=0):
    return dot1(a[0], b[0], ca, cb) + (dot1(a[0], b[1], ca, cb) + dot1(a[1], b[0], ca, cb))


def rows3(a, b, ca=1, cb=0):
    n = a[0].shape[0]
    both = dot1(jnp.concatenate(a, axis=0), b[0], ca, cb)
    return both[:n] + (both[n:] + dot1(a[0], b[1], ca, cb))


def dot6(a, b, ca=1, cb=0):
    return lax.dot_general(
        a, b, (((ca,), (cb,)), ((), ())), precision=lax.Precision.HIGHEST, preferred_element_type=f32
    )


def eye():
    return (lax.broadcasted_iota(jnp.int32, (R, R), 0) == lax.broadcasted_iota(jnp.int32, (R, R), 1)).astype(f32)


def sum_sq(x):
    return jnp.sum(x * x)


def sweep_inverse(ref):
    lane = lax.broadcasted_iota(jnp.int32, (1, R), 1)
    row_at = lax.broadcasted_iota(jnp.int32, (R, 1), 0)

    def body(k, _):
        a = ref[...]
        row = ref[pl.ds(k, 1), :]
        here = lane == k
        pivot = jnp.sum(jnp.where(here, row, 0.0), axis=1, keepdims=True)
        col = jnp.sum(jnp.where(here, a, 0.0), axis=1, keepdims=True)
        col = jnp.where(row_at == k, 0.0, col)
        row = jnp.where(here, 1.0, row) / pivot
        ref[...] = jnp.where(here, 0.0, a) - col * row
        ref[pl.ds(k, 1), :] = row
        return 0

    lax.fori_loop(0, R, body, 0)


ROWS = 24
INFO = 640


def partials(tm_ref, obs_ref, load_ref, noise_ref, out_ref):
    noise = noise_ref[...]
    column = jnp.broadcast_to(noise, (128, R)).T

    def weighted(i):
        return split(load_ref[:, 128 * i : 128 * i + 128].astype(f32) * column)

    def pairs(i, lo, at):
        rows = load_ref[:, lo:]
        hi, rest = weighted(i)
        blocks = dot1(hi, rows, 0, 0) + dot1(rest, rows, 0, 0)
        for n in range((R - lo) // 128):
            out_ref[at + 128 * n : at + 128 * n + 128, :] = blocks[:, 128 * n : 128 * n + 128]

    def one(i, at):
        rows = load_ref[:, 128 * i : 128 * i + 128]
        hi, rest = weighted(i)
        out_ref[at : at + 128, :] = dot1(hi, rows, 0, 0) + dot1(rest, rows, 0, 0)

    first = lax.rem(tm_ref[0], 2) == 0

    @pl.when(first)
    def _():
        pairs(0, 0, 0)
        one(1, 512)

    @pl.when(jnp.logical_not(first))
    def _():
        pairs(1, 256, 0)
        pairs(2, 256, 256)
        one(3, 512)

    hi, rest = split(obs_ref[...] * noise)
    rows = load_ref[...]
    info = dot1(hi, rows) + dot1(rest, rows)
    for t in range(4):
        for c in range(4):
            out_ref[INFO + 4 * t + c : INFO + 4 * t + c + 1, :] = info[t : t + 1, 128 * c : 128 * c + 128]
    out_ref[INFO + 16 :, :] = jnp.zeros((32 * ROWS - INFO - 16, 128), f32)


def prep_a(dyn_ref, prior_ref, wt_ref, nn_ref, q_ref, x_ref):
    prior = prior_ref[...]
    psplit = split(prior)
    wt = dot6(dyn_ref[...], prior, 0, 0)
    wt_ref[...] = wt
    nn = dot6(wt, dyn_ref[...])
    nn_ref[...] = nn
    q_ref[...] = prior - nn
    col = jnp.sum(jnp.abs(prior), axis=0, keepdims=True)
    start = 1.0 / jnp.max(col, axis=1, keepdims=True)
    ident = eye()
    x = ident * start
    ph = psplit[0]
    x = start * (2.0 * ident - start * prior)
    x_ref[...] = x

    def body(k, _):
        x = x_ref[...]
        xh = x.astype(bf16)
        t = dot1(ph, xh)
        x_ref[...] = 2.0 * x - dot1(xh, t.astype(bf16))
        return 0

    lax.fori_loop(0, 6, body, 0)


def refine(times_mat, x_ref, r_ref, done2, cap, product):
    ident = eye()

    def residual():
        r = ident - times_mat(x_ref[...])
        r_ref[...] = r
        return sum_sq(r)

    def cond(c):
        k, n2, old = c
        return (n2 > done2) & (k < cap) & (n2 < 0.98 * old)

    def body(c):
        k, n2, _ = c
        x = x_ref[...]
        x_ref[...] = x + product(x, r_ref[...])
        return k + 1, residual(), n2

    n0 = residual()
    return lax.while_loop(cond, body, (jnp.int32(0), n0, jnp.float32(jnp.inf)))[1]


def coarse(a, b):
    return dot1(a.astype(bf16), b.astype(bf16))


def fine(a, b):
    return dot3(split(a), split(b))


def prep_b(prior_ref, dyn_ref, x_in, x_ref, rest_ref, wp_ref, c_ref, r_ref):
    x_ref[...] = x_in[...]
    n2 = refine(lambda v: fine(prior_ref[...], v), x_ref, r_ref, 1e-5, 40, coarse)

    @pl.when(jnp.logical_not(n2 < 1e-3))
    def _():
        x_ref[...] = x_in[...]
        n2 = refine(lambda v: dot6(prior_ref[...], v), x_ref, r_ref, 1e-5, 40, fine)

        @pl.when(jnp.logical_not(n2 < 1e-2))
        def _():
            x_ref[...] = prior_ref[...]
            sweep_inverse(x_ref)

    rest = eye() - dot6(prior_ref[...], x_ref[...])
    rest_ref[...] = rest.astype(bf16)
    turned = dyn_ref[...].T
    wp_ref[...] = turned - coarse(turned, rest)
    mean = jnp.sum(jnp.sum(turned * eye(), axis=0, keepdims=True), axis=1, keepdims=True) * (1.0 / R)
    c_ref[...] = jnp.broadcast_to(mean, (8, 128))


PAIRS = ((0, 0), (0, 1), (0, 2), (0, 3), (1, 1), (1, 2), (1, 3), (2, 2), (2, 3), (3, 3))


def copies(sources, targets, sems):
    return [pltpu.make_async_copy(a, b, sems.at[n]) for n, (a, b) in enumerate(zip(sources, targets))]


def invert(tm_ref, *refs):
    sources, results, held, made, (g_ref, r_ref, sems, out_sems) = refs[2:8], refs[8:11], refs[11:17], refs[17:20], refs[20:]
    own_ref, other_ref = refs[:2]
    pinv_ref, rest_ref, wp_ref, q_ref, prior_ref, wt_ref = held
    x_ref, ft_ref, m_ref = made
    loads = copies(sources, held, sems)
    stores = copies(made, results, out_sems)
    for c in loads[:4]:
        c.start()
    first = lax.rem(tm_ref[0], 2) == 0
    for n, (i, j) in enumerate(PAIRS):
        at = (n % 5) * 128
        mine, theirs = own_ref[at : at + 128, :], other_ref[at : at + 128, :]
        blk = jnp.where(first, mine, theirs) if n < 5 else jnp.where(first, theirs, mine)
        g_ref[128 * i : 128 * i + 128, 128 * j : 128 * j + 128] = blk
        if i != j:
            g_ref[128 * j : 128 * j + 128, 128 * i : 128 * i + 128] = blk.T
    gram = g_ref[...]
    loads[0].wait()
    loads[1].wait()
    psplit = split(pinv_ref[...])
    h = dot3(split(gram), psplit) - rest_ref[...].astype(f32)
    h0, h1 = split(h)
    r = (h0.astype(f32) - h) + (dot1(h0, h0) + dot1(h1, h0))
    rh = r.astype(bf16)
    rr = dot1(rh, rh)
    n4 = sum_sq(rr)
    r = r + rr + dot1(rh, rr.astype(bf16))
    s = r - h0.astype(f32) - dot1(h0, r.astype(bf16))
    ss = split(s)
    loads[2].wait()
    loads[3].wait()
    m_ref[...] = gram + q_ref[...]
    stores[2].start()
    wp = wp_ref[...]
    good = n4 < 1e-6

    @pl.when(good)
    def _():
        x_ref[...] = pinv_ref[...] + dot3(psplit, ss)
        stores[0].start()
        ft_ref[...] = wp + dot3(split(wp), ss)
        stores[1].start()

    @pl.when(jnp.logical_not(good))
    def _():
        for c in loads[4:]:
            c.start()
            c.wait()
        e = coarse(g_ref[...], pinv_ref[...])
        theta = 2.0 / (2.0 + jnp.sqrt(sum_sq(e)))
        x_ref[...] = theta * pinv_ref[...]
        n2 = refine(lambda v: dot6(prior_ref[...] + g_ref[...], v), x_ref, r_ref, 1e-9, 60, fine)

        @pl.when(jnp.logical_not(n2 < 1e-6))
        def _():
            x_ref[...] = prior_ref[...] + g_ref[...]
            sweep_inverse(x_ref)

        ft_ref[...] = dot6(wt_ref[...], x_ref[...])
        stores[0].start()
        stores[1].start()

    for c in stores:
        c.wait()


def scans(tm_ref, *refs):
    sources, (filt_ref, smooth_ref), held, (f_ref, s_ref, sems) = refs[:6], refs[6:8], refs[8:14], refs[14:]
    ft_ref, info_ref, x_ref, m_ref, nn_ref, c_ref = held
    loads = copies(sources, held, sems)
    for c in loads[5:] + loads[:5]:
        c.start()
    T = 64
    loads[0].wait()
    loads[5].wait()
    f = ft_ref[...]
    powers = [split(f)]
    c = c_ref[0:1, 0:1]
    e = f - c * eye()
    es = split(e)
    f = c * (f + e) + dot3(es, es)
    powers.append(split(f))
    loads[1].wait()
    loads[2].wait()
    x = split(x_ref[...])
    parts = [info_ref[pl.ds(c, T, stride=4), :] for c in range(4)]
    info = jnp.concatenate(parts, axis=1)
    y = rows3(split(info), x)
    for _ in range(3):
        f = dot3(powers[-1], powers[-1])
        powers.append(split(f))
    leap = powers.pop()
    step = lax.broadcasted_iota(jnp.int32, (T, 1), 0)

    def later(v, k):
        return jnp.where(step >= k, pltpu.roll(v, k, 0), 0.0)

    def sooner(v, k):
        return jnp.where(step < T - k, pltpu.roll(v, T - k, 0), 0.0)

    for n, p in enumerate(powers):
        y = y + later(rows3(split(y), p), 1 << n)
    blocks = [y[16 * b : 16 * b + 16] for b in range(4)]
    for b in range(1, 4):
        blocks[b] = blocks[b] + rows3(split(blocks[b - 1]), leap)
    y = jnp.concatenate(blocks, axis=0)
    f_ref[...] = y
    loads[3].wait()
    loads[4].wait()
    nn = nn_ref[...]
    ys = split(y)
    u = rows3(ys, split(m_ref[...]))
    tail = dot3(split(y[T - 8 :, :]), split(nn))
    u = u + jnp.where(step == T - 1, jnp.concatenate([jnp.zeros((T - 8, R), f32), tail], axis=0), 0.0)
    for n, p in enumerate(powers):
        u = u + sooner(rows3(split(u), p, 1, 1), 1 << n)
    blocks = [u[16 * b : 16 * b + 16] for b in range(4)]
    for b in range(2, -1, -1):
        blocks[b] = blocks[b] + rows3(split(blocks[b + 1]), leap, 1, 1)
    u = jnp.concatenate(blocks, axis=0)
    s_ref[...] = rows3(split(u), x)
    at = pl.multiple_of(8 * lax.div(tm_ref[0], 2), 8)
    half = lax.rem(tm_ref[0], 2) == 0
    fb = f_ref[pl.ds(at, 8), :]
    sb = s_ref[pl.ds(at, 8), :]
    filt_ref[...] = jnp.where(half, fb[0:4], fb[4:8])
    smooth_ref[...] = jnp.where(half, sb[0:4], sb[4:8])


vm = partial(pltpu.VMEM, (R, R), f32)
mat = jax.ShapeDtypeStruct((R, R), f32)
half = jax.ShapeDtypeStruct((R, R), bf16)
tile = jax.ShapeDtypeStruct((8, 128), f32)
smem = pl.BlockSpec(memory_space=pltpu.SMEM)
vmem = pl.BlockSpec(memory_space=pltpu.VMEM)
room = pltpu.CompilerParams(vmem_limit_bytes=28 << 20)


anywhere = pl.BlockSpec(memory_space=pl.ANY)
far = pltpu.HBM((R, R), f32)


def near(arrays):
    return [pltpu.with_memory_space_constraint(a, pltpu.VMEM) for a in arrays]


def kept_far(arrays):
    return [pltpu.with_memory_space_constraint(a, pltpu.HBM) for a in arrays]

part = pltpu.VMEM((32 * ROWS, 128), f32)


def prep_first(dyn, prior):
    return pl.pallas_call(prep_a, out_shape=(mat,) * 4, name="prep_a")(dyn, prior)


def prep_second(prior, dyn, x):
    return pl.pallas_call(prep_b, out_shape=(mat, half, mat, tile), scratch_shapes=[vm()], name="prep_b")(prior, dyn, x)


def inverse(tm, *arrays):
    dma = pltpu.SemaphoreType.DMA
    return pl.pallas_call(
        invert,
        out_shape=(far, far, far),
        in_specs=[smem] + [vmem] * 2 + [anywhere] * 6,
        out_specs=(anywhere,) * 3,
        scratch_shapes=[vm(), pltpu.VMEM((R, R), bf16)] + [vm()] * 9 + [dma((6,)), dma((3,))],
        name="invert",
        compiler_params=room,
    )(tm, *near(arrays[:2]), *kept_far(arrays[2:]))


def time_scans(tm, *arrays):
    out = jax.ShapeDtypeStruct((4, R), f32)
    rows = pltpu.VMEM((64, R), f32)
    return pl.pallas_call(
        scans,
        out_shape=(out, out),
        in_specs=[smem] + [anywhere] * 6,
        scratch_shapes=[vm(), pltpu.VMEM((256, 128), f32), vm(), vm(), vm(), pltpu.VMEM((8, 128), f32), rows, rows, pltpu.SemaphoreType.DMA((6,))],
        name="scans",
        compiler_params=room,
    )(tm, *kept_far(arrays[:1]), arrays[1], *kept_far(arrays[2:]))


def local_partials(tm, observed, loadings, noise):
    return pl.pallas_call(
        partials,
        out_shape=jax.ShapeDtypeStruct((32 * ROWS, 128), f32),
        in_specs=[smem] + [vmem] * 3,
        name="partials",
    )(tm, observed, loadings, noise)


def exchange(pieces, axis):
    return lax.all_to_all(pieces, axis, split_axis=0, concat_axis=0, tiled=True)


def shards(observed, loadings, noise_prec, dynamics, prior_prec):
    tm = lax.axis_index("tm").astype(jnp.int32).reshape(1)
    send = local_partials(tm, observed, loadings, noise_prec.reshape(1, R))
    send, dynamics, prior_prec = lax.optimization_barrier((send, dynamics, prior_prec))
    pieces = exchange(send.reshape(32, ROWS, 128), "sens")
    wt, nn, q, x0 = prep_first(dynamics, prior_prec)
    total = jnp.broadcast_to(pieces.sum(axis=0), pieces.shape)
    total, x0 = lax.optimization_barrier((total, x0))
    own = exchange(total, "sens").reshape(32 * ROWS, 128)
    pinv, rest, wp, c = prep_second(prior_prec, dynamics, x0)
    own, pinv = lax.optimization_barrier((own, pinv))
    other = lax.ppermute(own, "tm", [(i, i ^ 1) for i in range(16)])
    info = jnp.broadcast_to(own[INFO : INFO + 16], (16, 16, 128))
    info = exchange(info, "tm").reshape(256, 128)
    x, ft, m = inverse(tm, own, other, pinv, rest, wp, q, prior_prec, wt)
    return time_scans(tm, ft, info, x, m, nn, c)


def solution(mesh):
    return jax.shard_map(
        shards,
        mesh=mesh,
        in_specs=(P("tm", "sens"), P("sens", None), P("sens"), P(), P()),
        out_specs=(P("tm", None), P("tm", None)),
        check_vma=False,
    )
```

```python
from functools import partial

import jax
import jax.numpy as jnp
from jax import lax
from jax.experimental import pallas as pl
from jax.experimental.pallas import tpu as pltpu
from jax.sharding import PartitionSpec as P

f32 = jnp.float32
bf16 = jnp.bfloat16
R = 512


def dot1(a, b, ca=1, cb=0):
    return lax.dot_general(a, b, (((ca,), (cb,)), ((), ())), preferred_element_type=f32)


def split(a):
    hi = a.astype(bf16)
    return hi, (a - hi.astype(f32)).astype(bf16)


def dot3(a, b, ca=1, cb=0):
    return dot1(a[0], b[0], ca, cb) + (dot1(a[0], b[1], ca, cb) + dot1(a[1], b[0], ca, cb))


def rows3(a, b, ca=1, cb=0):
    n = a[0].shape[0]
    both = dot1(jnp.concatenate(a, axis=0), b[0], ca, cb)
    return both[:n] + (both[n:] + dot1(a[0], b[1], ca, cb))


def dot6(a, b, ca=1, cb=0):
    return lax.dot_general(
        a, b, (((ca,), (cb,)), ((), ())), precision=lax.Precision.HIGHEST, preferred_element_type=f32
    )


def eye():
    return (lax.broadcasted_iota(jnp.int32, (R, R), 0) == lax.broadcasted_iota(jnp.int32, (R, R), 1)).astype(f32)


def sum_sq(x):
    return jnp.sum(x * x)


def sweep_inverse(ref):
    lane = lax.broadcasted_iota(jnp.int32, (1, R), 1)
    row_at = lax.broadcasted_iota(jnp.int32, (R, 1), 0)

    def body(k, _):
        a = ref[...]
        row = ref[pl.ds(k, 1), :]
        here = lane == k
        pivot = jnp.sum(jnp.where(here, row, 0.0), axis=1, keepdims=True)
        col = jnp.sum(jnp.where(here, a, 0.0), axis=1, keepdims=True)
        col = jnp.where(row_at == k, 0.0, col)
        row = jnp.where(here, 1.0, row) / pivot
        ref[...] = jnp.where(here, 0.0, a) - col * row
        ref[pl.ds(k, 1), :] = row
        return 0

    lax.fori_loop(0, R, body, 0)


ROWS = 24
INFO = 640


def partials(tm_ref, obs_ref, load_ref, noise_ref, out_ref):
    noise = noise_ref[...]
    column = jnp.broadcast_to(noise, (128, R)).T

    def weighted(i):
        return split(load_ref[:, 128 * i : 128 * i + 128].astype(f32) * column)

    def pairs(i, lo, at):
        rows = load_ref[:, lo:]
        hi, rest = weighted(i)
        blocks = dot1(hi, rows, 0, 0) + dot1(rest, rows, 0, 0)
        for n in range((R - lo) // 128):
            out_ref[at + 128 * n : at + 128 * n + 128, :] = blocks[:, 128 * n : 128 * n + 128]

    def one(i, at):
        rows = load_ref[:, 128 * i : 128 * i + 128]
        hi, rest = weighted(i)
        out_ref[at : at + 128, :] = dot1(hi, rows, 0, 0) + dot1(rest, rows, 0, 0)

    first = lax.rem(tm_ref[0], 2) == 0

    @pl.when(first)
    def _():
        pairs(0, 0, 0)
        one(1, 512)

    @pl.when(jnp.logical_not(first))
    def _():
        pairs(1, 256, 0)
        pairs(2, 256, 256)
        one(3, 512)

    hi, rest = split(obs_ref[...] * noise)
    rows = load_ref[...]
    info = dot1(hi, rows) + dot1(rest, rows)
    for t in range(4):
        for c in range(4):
            out_ref[INFO + 4 * t + c : INFO + 4 * t + c + 1, :] = info[t : t + 1, 128 * c : 128 * c + 128]
    out_ref[INFO + 16 :, :] = jnp.zeros((32 * ROWS - INFO - 16, 128), f32)


def prep_a(dyn_ref, prior_ref, wt_ref, nn_ref, q_ref, x_ref):
    prior = prior_ref[...]
    psplit = split(prior)
    wt = dot6(dyn_ref[...], prior, 0, 0)
    wt_ref[...] = wt
    nn = dot6(wt, dyn_ref[...])
    nn_ref[...] = nn
    q_ref[...] = prior - nn
    col = jnp.sum(jnp.abs(prior), axis=0, keepdims=True)
    start = 1.0 / jnp.max(col, axis=1, keepdims=True)
    ident = eye()
    x = ident * start
    ph = psplit[0]
    x = start * (2.0 * ident - start * prior)
    x_ref[...] = x

    def body(k, _):
        x = x_ref[...]
        xh = x.astype(bf16)
        t = dot1(ph, xh)
        x_ref[...] = 2.0 * x - dot1(xh, t.astype(bf16))
        return 0

    lax.fori_loop(0, 6, body, 0)


def refine(times_mat, x_ref, r_ref, done2, cap, product):
    ident = eye()

    def residual():
        r = ident - times_mat(x_ref[...])
        r_ref[...] = r
        return sum_sq(r)

    def cond(c):
        k, n2, old = c
        return (n2 > done2) & (k < cap) & (n2 < 0.98 * old)

    def body(c):
        k, n2, _ = c
        x = x_ref[...]
        x_ref[...] = x + product(x, r_ref[...])
        return k + 1, residual(), n2

    n0 = residual()
    return lax.while_loop(cond, body, (jnp.int32(0), n0, jnp.float32(jnp.inf)))[1]


def coarse(a, b):
    return dot1(a.astype(bf16), b.astype(bf16))


def fine(a, b):
    return dot3(split(a), split(b))


def prep_b(prior_ref, dyn_ref, x_in, x_ref, rest_ref, wp_ref, c_ref, r_ref):
    x_ref[...] = x_in[...]
    n2 = refine(lambda v: fine(prior_ref[...], v), x_ref, r_ref, 1e-5, 40, coarse)

    @pl.when(jnp.logical_not(n2 < 1e-3))
    def _():
        x_ref[...] = x_in[...]
        n2 = refine(lambda v: dot6(prior_ref[...], v), x_ref, r_ref, 1e-5, 40, fine)

        @pl.when(jnp.logical_not(n2 < 1e-2))
        def _():
            x_ref[...] = prior_ref[...]
            sweep_inverse(x_ref)

    rest = eye() - dot6(prior_ref[...], x_ref[...])
    rest_ref[...] = rest.astype(bf16)
    turned = dyn_ref[...].T
    wp_ref[...] = turned - coarse(turned, rest)
    mean = jnp.sum(jnp.sum(turned * eye(), axis=0, keepdims=True), axis=1, keepdims=True) * (1.0 / R)
    c_ref[...] = jnp.broadcast_to(mean, (8, 128))


PAIRS = ((0, 0), (0, 1), (0, 2), (0, 3), (1, 1), (1, 2), (1, 3), (2, 2), (2, 3), (3, 3))


def copies(sources, targets, sems):
    return [pltpu.make_async_copy(a, b, sems.at[n]) for n, (a, b) in enumerate(zip(sources, targets))]


def invert(tm_ref, *refs):
    sources, results, held, made, (g_ref, r_ref, sems, out_sems) = refs[2:8], refs[8:11], refs[11:17], refs[17:20], refs[20:]
    own_ref, other_ref = refs[:2]
    pinv_ref, rest_ref, wp_ref, q_ref, prior_ref, wt_ref = held
    x_ref, ft_ref, m_ref = made
    loads = copies(sources, held, sems)
    stores = copies(made, results, out_sems)
    for c in loads[:4]:
        c.start()
    first = lax.rem(tm_ref[0], 2) == 0
    for n, (i, j) in enumerate(PAIRS):
        at = (n % 5) * 128
        mine, theirs = own_ref[at : at + 128, :], other_ref[at : at + 128, :]
        blk = jnp.where(first, mine, theirs) if n < 5 else jnp.where(first, theirs, mine)
        g_ref[128 * i : 128 * i + 128, 128 * j : 128 * j + 128] = blk
        if i != j:
            g_ref[128 * j : 128 * j + 128, 128 * i : 128 * i + 128] = blk.T
    gram = g_ref[...]
    loads[0].wait()
    loads[1].wait()
    psplit = split(pinv_ref[...])
    h = dot3(split(gram), psplit) - rest_ref[...].astype(f32)
    h0, h1 = split(h)
    r = (h0.astype(f32) - h) + (dot1(h0, h0) + dot1(h1, h0))
    rh = r.astype(bf16)
    rr = dot1(rh, rh)
    n4 = sum_sq(rr)
    r = r + rr + dot1(rh, rr.astype(bf16))
    s = r - h0.astype(f32) - dot1(h0, r.astype(bf16))
    ss = split(s)
    loads[2].wait()
    loads[3].wait()
    m_ref[...] = gram + q_ref[...]
    stores[2].start()
    wp = wp_ref[...]
    good = n4 < 1e-6

    @pl.when(good)
    def _():
        x_ref[...] = pinv_ref[...] + dot3(psplit, ss)
        stores[0].start()
        ft_ref[...] = wp + dot3(split(wp), ss)
        stores[1].start()

    @pl.when(jnp.logical_not(good))
    def _():
        for c in loads[4:]:
            c.start()
            c.wait()
        e = coarse(g_ref[...], pinv_ref[...])
        theta = 2.0 / (2.0 + jnp.sqrt(sum_sq(e)))
        x_ref[...] = theta * pinv_ref[...]
        n2 = refine(lambda v: dot6(prior_ref[...] + g_ref[...], v), x_ref, r_ref, 1e-9, 60, fine)

        @pl.when(jnp.logical_not(n2 < 1e-6))
        def _():
            x_ref[...] = prior_ref[...] + g_ref[...]
            sweep_inverse(x_ref)

        ft_ref[...] = dot6(wt_ref[...], x_ref[...])
        stores[0].start()
        stores[1].start()

    for c in stores:
        c.wait()


def scans(tm_ref, *refs):
    sources, (filt_ref, smooth_ref), held, (f_ref, s_ref, sems) = refs[:6], refs[6:8], refs[8:14], refs[14:]
    ft_ref, info_ref, x_ref, m_ref, nn_ref, c_ref = held
    loads = copies(sources, held, sems)
    for c in loads[5:] + loads[:5]:
        c.start()
    T = 64
    loads[0].wait()
    loads[5].wait()
    f = ft_ref[...]
    powers = [split(f)]
    c = c_ref[0:1, 0:1]
    e = f - c * eye()
    es = split(e)
    f = c * (f + e) + dot3(es, es)
    powers.append(split(f))
    loads[1].wait()
    loads[2].wait()
    x = split(x_ref[...])
    parts = [info_ref[pl.ds(c, T, stride=4), :] for c in range(4)]
    info = jnp.concatenate(parts, axis=1)
    y = rows3(split(info), x)
    for _ in range(3):
        f = dot3(powers[-1], powers[-1])
        powers.append(split(f))
    leap = powers.pop()
    step = lax.broadcasted_iota(jnp.int32, (T, 1), 0)

    def later(v, k):
        return jnp.where(step >= k, pltpu.roll(v, k, 0), 0.0)

    def sooner(v, k):
        return jnp.where(step < T - k, pltpu.roll(v, T - k, 0), 0.0)

    for n, p in enumerate(powers):
        y = y + later(rows3(split(y), p), 1 << n)
    blocks = [y[16 * b : 16 * b + 16] for b in range(4)]
    for b in range(1, 4):
        blocks[b] = blocks[b] + rows3(split(blocks[b - 1]), leap)
    y = jnp.concatenate(blocks, axis=0)
    f_ref[...] = y
    loads[3].wait()
    loads[4].wait()
    nn = nn_ref[...]
    ys = split(y)
    u = rows3(ys, split(m_ref[...]))
    tail = dot3(split(y[T - 8 :, :]), split(nn))
    u = u + jnp.where(step == T - 1, jnp.concatenate([jnp.zeros((T - 8, R), f32), tail], axis=0), 0.0)
    for n, p in enumerate(powers):
        u = u + sooner(rows3(split(u), p, 1, 1), 1 << n)
    blocks = [u[16 * b : 16 * b + 16] for b in range(4)]
    for b in range(2, -1, -1):
        blocks[b] = blocks[b] + rows3(split(blocks[b + 1]), leap, 1, 1)
    u = jnp.concatenate(blocks, axis=0)
    s_ref[...] = rows3(split(u), x)
    at = pl.multiple_of(8 * lax.div(tm_ref[0], 2), 8)
    half = lax.rem(tm_ref[0], 2) == 0
    fb = f_ref[pl.ds(at, 8), :]
    sb = s_ref[pl.ds(at, 8), :]
    filt_ref[...] = jnp.where(half, fb[0:4], fb[4:8])
    smooth_ref[...] = jnp.where(half, sb[0:4], sb[4:8])


vm = partial(pltpu.VMEM, (R, R), f32)
mat = jax.ShapeDtypeStruct((R, R), f32)
half = jax.ShapeDtypeStruct((R, R), bf16)
tile = jax.ShapeDtypeStruct((8, 128), f32)
smem = pl.BlockSpec(memory_space=pltpu.SMEM)
vmem = pl.BlockSpec(memory_space=pltpu.VMEM)
room = pltpu.CompilerParams(vmem_limit_bytes=28 << 20)


anywhere = pl.BlockSpec(memory_space=pl.ANY)
far = pltpu.HBM((R, R), f32)


def near(arrays):
    return [pltpu.with_memory_space_constraint(a, pltpu.VMEM) for a in arrays]


def kept_far(arrays):
    return [pltpu.with_memory_space_constraint(a, pltpu.HBM) for a in arrays]

part = pltpu.VMEM((32 * ROWS, 128), f32)


def prep_first(dyn, prior):
    return pl.pallas_call(prep_a, out_shape=(mat,) * 4, name="prep_a")(dyn, prior)


def prep_second(prior, dyn, x):
    return pl.pallas_call(prep_b, out_shape=(mat, half, mat, tile), scratch_shapes=[vm()], name="prep_b")(prior, dyn, x)


def inverse(tm, *arrays):
    dma = pltpu.SemaphoreType.DMA
    return pl.pallas_call(
        invert,
        out_shape=(far, far, far),
        in_specs=[smem] + [vmem] * 2 + [anywhere] * 6,
        out_specs=(anywhere,) * 3,
        scratch_shapes=[vm(), pltpu.VMEM((R, R), bf16)] + [vm()] * 9 + [dma((6,)), dma((3,))],
        name="invert",
        compiler_params=room,
    )(tm, *near(arrays[:2]), *kept_far(arrays[2:]))


def time_scans(tm, *arrays):
    out = jax.ShapeDtypeStruct((4, R), f32)
    rows = pltpu.VMEM((64, R), f32)
    return pl.pallas_call(
        scans,
        out_shape=(out, out),
        in_specs=[smem] + [anywhere] * 6,
        scratch_shapes=[vm(), pltpu.VMEM((256, 128), f32), vm(), vm(), vm(), pltpu.VMEM((8, 128), f32), rows, rows, pltpu.SemaphoreType.DMA((6,))],
        name="scans",
        compiler_params=room,
    )(tm, *kept_far(arrays[:1]), arrays[1], *kept_far(arrays[2:5]), arrays[5])


def local_partials(tm, observed, loadings, noise):
    return pl.pallas_call(
        partials,
        out_shape=jax.ShapeDtypeStruct((32 * ROWS, 128), f32),
        in_specs=[smem] + [vmem] * 3,
        name="partials",
    )(tm, observed, loadings, noise)


def exchange(pieces, axis):
    return lax.all_to_all(pieces, axis, split_axis=0, concat_axis=0, tiled=True)


def shards(observed, loadings, noise_prec, dynamics, prior_prec):
    tm = lax.axis_index("tm").astype(jnp.int32).reshape(1)
    send = local_partials(tm, observed, loadings, noise_prec.reshape(1, R))
    send, dynamics, prior_prec = lax.optimization_barrier((send, dynamics, prior_prec))
    pieces = exchange(send.reshape(32, ROWS, 128), "sens")
    wt, nn, q, x0 = prep_first(dynamics, prior_prec)
    total = jnp.broadcast_to(pieces.sum(axis=0), pieces.shape)
    total, x0 = lax.optimization_barrier((total, x0))
    own = exchange(total, "sens").reshape(32 * ROWS, 128)
    pinv, rest, wp, c = prep_second(prior_prec, dynamics, x0)
    own, pinv = lax.optimization_barrier((own, pinv))
    other = lax.ppermute(own, "tm", [(i, i ^ 1) for i in range(16)])
    info = jnp.broadcast_to(own[INFO : INFO + 16], (16, 16, 128))
    info = exchange(info, "tm").reshape(256, 128)
    x, ft, m = inverse(tm, own, other, pinv, rest, wp, q, prior_prec, wt)
    return time_scans(tm, ft, info, x, m, nn, c)


def solution(mesh):
    return jax.shard_map(
        shards,
        mesh=mesh,
        in_specs=(P("tm", "sens"), P("sens", None), P("sens"), P(), P()),
        out_specs=(P("tm", None), P("tm", None)),
        check_vma=False,
    )
```
